32 devices in a mesh: queue: 8 (over z, core), tok: 4 (over y, x).
Axes of the slice: x: 2, y: 2, z: 4, core: 2. Of those that a mesh axis runs over, the one named last changes fastest.
Arguments:
- latents: float32 [8, 512, 64], P('queue', 'tok'), may hold values from -6 to 6
- step_index: int32 [8], replicated, may hold values from 0 to 31, as said below
- tail_noise: float32 [512, 64], P('tok'), may hold values from -6 to 6
- patch_weight: bfloat16 [64, 1536], replicated, may hold values from -0.75 to 0.75
- time_table: float32 [32, 3, 1536], replicated, may hold values from -3 to 3
- qkv_weight: bfloat16 [1536, 4608], replicated, may hold values from -1 to 1
- q_gain: float32 [1536], replicated, may hold values from 1 to 3
- k_gain: float32 [1536], replicated, may hold values from 1 to 3
- out_weight: bfloat16 [1536, 1536], replicated, may hold values from -0.15625 to 0.15625
- head_weight: bfloat16 [1536, 64], replicated, may hold values from -0.15625 to 0.15625
Outputs:
- velocity: float32 [8, 512, 64], P('queue', 'tok')
- queue_next: float32 [8, 512, 64], P('queue', 'tok')
- leaving: float32 [64, 512], P('queue', 'tok')
The draws below stay inside these ranges and needn't reach their ends.
Inputs may be any that keep to these rules, and one draw needn't show every extreme that they name: `step_index`: strictly rising along the queue, by 1 to 4 from one frame to the next; the tail frame is at level 31.
All inputs are finite; a program needn't handle non-finite values.
Results may differ from the reference program's by a relative error of at most 0.0095.
Values may be sent and summed in bfloat16 or wider, within the bound.
No kernel may reach another device: no remote copies, remote signals or barrier semaphores. Data moves between devices by JAX's collectives and lax.ppermute only.
A program may use at most 320 MiB of HBM per device.

```python
import math
import jax
import jax.numpy as jnp
from jax import lax

D = 1536
HEADS = 12
HEAD_DIM = 128
C = 64
FRAMES = 8
TOKF = 512
LEVELS = 32


def draw_step_index(key, part):
    strides = jax.random.randint(jax.random.fold_in(key, 12), (FRAMES - 1,), 1, 5).astype(jnp.int32)
    opening = (LEVELS - 1 - jnp.sum(strides)).astype(jnp.int32)
    rising = jnp.concatenate([jnp.zeros((1,), jnp.int32), jnp.cumsum(strides).astype(jnp.int32)])
    return (opening + rising).astype(jnp.int32)


def draw_qkv_weight(key, part):
    base = jax.random.normal(jax.random.fold_in(key, 21), (D, 3 * D), jnp.float32) * D ** (-0.5)
    base = jnp.clip(base, -1.0, 1.0)
    return base.astype(jnp.bfloat16)


def level_of(own_key, shape, cuts, low, top_value):
    gain, own = 1.0, jax.random.fold_in(own_key, 6)
    for position, parts in cuts:
        draws = jnp.exp(jax.random.uniform(jax.random.fold_in(own, position), (parts,), jnp.float32, low / len(cuts), top_value / len(cuts)))
        gain = gain * jnp.repeat(draws, shape[position] // parts).reshape([-1 if axis == position else 1 for axis in range(len(shape))])
    return gain


def gaussian(own_key, dims, width, bound, split=(), kind=jnp.bfloat16):
    entries = jax.random.normal(own_key, dims, jnp.float32) * width
    if len(split) > 0:
        entries = level_of(own_key, dims, split, -0.22, 0.18) * entries
    return jnp.clip(entries, min=-bound, max=bound).astype(kind)


def setup_inputs(seed: int = 0) -> dict:
    key_list = jax.random.split(jax.random.key(seed), 11)
    latents = gaussian(key_list[0], (FRAMES, TOKF, C), 1.0, 6.0, ((0, 8), (1, 4)), jnp.float32)
    step_index = draw_step_index(jax.random.fold_in(key_list[10], 71), 0)
    tail_noise = gaussian(key_list[2], (TOKF, C), 1.0, 6.0, ((0, 4),), jnp.float32)
    patch_weight = gaussian(key_list[3], (C, D), C ** -0.5, 0.75)
    time_table = gaussian(key_list[4], (LEVELS, 3, D), 0.5, 3.0, (), jnp.float32)
    qkv_weight = draw_qkv_weight(jax.random.fold_in(key_list[10], 71), 0)
    q_gain = jnp.clip(jnp.exp(jax.random.uniform(key_list[6], (D,), jnp.float32, math.log(1.0), math.log(3.0))), 1.0, 3.0)
    k_gain = jnp.clip(jnp.exp(jax.random.uniform(key_list[7], (D,), jnp.float32, math.log(1.0), math.log(3.0))), 1.0, 3.0)
    out_weight = gaussian(key_list[8], (D, D), D ** -0.5, 0.15625)
    head_weight = gaussian(key_list[9], (D, C), D ** -0.5, 0.15625)
    return dict(latents=latents, step_index=step_index, tail_noise=tail_noise, patch_weight=patch_weight, time_table=time_table, qkv_weight=qkv_weight, q_gain=q_gain, k_gain=k_gain, out_weight=out_weight, head_weight=head_weight)


def layer_norm(values):
    mean_row = lax.optimization_barrier(jnp.mean(values, axis=-1, keepdims=True))
    centred = values - mean_row
    variance = lax.optimization_barrier(jnp.mean(centred * centred, axis=-1, keepdims=True))
    return centred * lax.rsqrt(variance + 1e-06)

def rms_norm(values, gain_vec):
    return values * lax.rsqrt(lax.optimization_barrier(jnp.mean(values * values, axis=-1, keepdims=True)) + 1e-06) * gain_vec

def widen(values):
    return lax.optimization_barrier(values).astype(jnp.float32)

def reference(latents, step_index, tail_noise, patch_weight, time_table, qkv_weight, q_gain, k_gain, out_weight, head_weight):
    one_hot = (step_index[:, None] == jnp.arange(LEVELS, dtype=jnp.int32)[None, :]).astype(jnp.float32)
    modulation = jnp.dot(one_hot, time_table.reshape(LEVELS, 3 * D), precision=lax.Precision.HIGHEST).reshape(FRAMES, 3, D)
    shift_vec = modulation[:, 0][:, None, :]
    scale_vec = modulation[:, 1][:, None, :]
    gate_vec = modulation[:, 2][:, None, :]
    hidden = jnp.dot(latents.reshape(FRAMES * TOKF, C).astype(jnp.bfloat16), patch_weight, preferred_element_type=jnp.float32).reshape(FRAMES, TOKF, D)
    normed = (layer_norm(hidden) * (1.0 + scale_vec) + shift_vec).astype(jnp.bfloat16)
    projected = jnp.dot(normed.reshape(FRAMES * TOKF, D), qkv_weight, preferred_element_type=jnp.float32)
    queries = rms_norm(projected[:, :D], q_gain).astype(jnp.bfloat16).reshape(FRAMES, TOKF, HEADS, HEAD_DIM)
    key_rows = rms_norm(projected[:, D:2 * D], k_gain).astype(jnp.bfloat16).reshape(FRAMES * TOKF, HEADS, HEAD_DIM)
    value_rows = projected[:, 2 * D:].astype(jnp.bfloat16).reshape(FRAMES * TOKF, HEADS, HEAD_DIM)
    all_keys = widen(key_rows)
    all_values = widen(value_rows)

    def one_frame(frame_idx):
        own_queries = widen(lax.dynamic_index_in_dim(queries, frame_idx, 0, keepdims=False))
        scores = jnp.einsum('qhd,khd->qhk', own_queries, all_keys) * HEAD_DIM ** (-0.5)
        weights = jnp.exp(scores - lax.optimization_barrier(jnp.max(scores, axis=-1, keepdims=True)))
        totals = lax.optimization_barrier(jnp.sum(weights, axis=-1))
        rounded = widen(weights.astype(jnp.bfloat16))
        attended = jnp.einsum('qhk,khd->qhd', rounded, all_values) / totals[..., None]
        return attended.reshape(TOKF, D).astype(jnp.bfloat16)
    attended = lax.map(one_frame, jnp.arange(FRAMES, dtype=jnp.int32))
    attn_out = jnp.dot(attended.reshape(FRAMES * TOKF, D), out_weight, preferred_element_type=jnp.float32).reshape(FRAMES, TOKF, D)
    residual = hidden + gate_vec * attn_out
    velocity = jnp.dot(residual.reshape(FRAMES * TOKF, D).astype(jnp.bfloat16), head_weight, preferred_element_type=jnp.float32).reshape(FRAMES, TOKF, C)
    level_before = jnp.concatenate([jnp.full((1,), -1, jnp.int32), step_index[:-1]])
    sigma_now = (step_index.astype(jnp.float32) + 1.0) / LEVELS
    sigma_next = (level_before.astype(jnp.float32) + 1.0) / LEVELS
    updated = latents + (sigma_next - sigma_now)[:, None, None] * velocity
    queue_next = jnp.concatenate([updated[1:], tail_noise[None]], axis=0)
    leaving = updated[0].T
    return (velocity, queue_next, leaving)
```

```python
import functools
import math

import jax
import jax.numpy as jnp
from jax import lax
from jax.experimental import pallas as pl
from jax.experimental.pallas import tpu as pltpu
from jax.sharding import PartitionSpec as P

HEAD_DIM = 128
EPS = 1e-06
UROWS = 80
GROUPS = 4
CHUNK = 256
EXACT = lax.Precision.HIGHEST
VMEM = pl.BlockSpec(memory_space=pltpu.VMEM)
SMEM = pl.BlockSpec(memory_space=pltpu.SMEM)
ANY = pl.BlockSpec(memory_space=pl.ANY)


def nt_dot(a, b, **kw):
    return lax.dot_general(a, b, (((1,), (1,)), ((), ())), preferred_element_type=jnp.float32, **kw)


def tn_dot(a, b, **kw):
    return lax.dot_general(a, b, (((0,), (0,)), ((), ())), preferred_element_type=jnp.float32, **kw)


def nn_dot(a, b, **kw):
    return jnp.dot(a, b, preferred_element_type=jnp.float32, **kw)


def frame_at(place, mine, frames):
    half = frames // 2
    return mine ^ (((place % half) << 1) | (place // half))


def place_of(frame, mine, frames):
    apart = mine ^ frame
    return (apart >> 1) + (apart & 1) * (frames // 2)


def query_frames(mine, frames):
    first = mine - (mine & 1)
    return (first, first + 1, jnp.minimum(first + 2, frames - 1), 0 * first)


def tables_kernel(
    frames,
    step_ref,
    time_ref,
    patch_ref,
    qkv_ref,
    q_gain_ref,
    k_gain_ref,
    out_ref,
    head_ref,
    ak_ref,
    av_ref,
    aq_ref,
    hk_ref,
    hq_ref,
    gram_ref,
    mix_ref,
    skip_ref,
    lhs,
    lhs_q,
    head_g,
    wbuf,
    obuf,
    sems,
):
    feature = patch_ref.shape[1]
    channels = patch_ref.shape[0]
    half = ak_ref.shape[2]
    mine = lax.axis_index("queue")
    core = mine & 1
    per_half = half // CHUNK
    whole = feature // CHUNK

    def column(j):
        return pl.multiple_of(lax.rem(core * half + j * CHUNK, feature), CHUNK)

    def fetch(slot, base, j):
        at = pl.multiple_of(base + column(j), CHUNK)
        return pltpu.make_async_copy(qkv_ref.at[:, pl.ds(at, CHUNK)], wbuf.at[slot], sems.at[slot])

    k_slot, v_slot, q_slot = 0, whole, whole + per_half
    for j in range(whole):
        fetch(k_slot + j, feature, j).start()
    for j in range(per_half):
        fetch(v_slot + j, 2 * feature, j).start()
    for j in range(whole):
        fetch(q_slot + j, 0, j).start()
    last = whole + per_half + whole
    out_copy = pltpu.make_async_copy(
        out_ref.at[pl.ds(pl.multiple_of(core * half, half), half), :], obuf, sems.at[last]
    )
    out_copy.start()

    patch = patch_ref[...].astype(jnp.float32)
    centred = patch - jnp.mean(patch, axis=-1, keepdims=True)
    gram_ref[...] = nt_dot(centred, centred, precision=EXACT) / feature
    rest = UROWS - channels
    first_row = lax.broadcasted_iota(jnp.int32, (rest, feature), 0) == 0
    for place in range(frames):
        level = step_ref[frame_at(place, mine, frames)]
        shift = time_ref[0, pl.ds(level, 1), :]
        scale = time_ref[1, pl.ds(level, 1), :]
        lhs[place * UROWS : place * UROWS + channels, :] = (centred * (1.0 + scale)).astype(jnp.bfloat16)
        lhs[place * UROWS + channels : (place + 1) * UROWS, :] = jnp.where(
            first_row, jnp.broadcast_to(shift, (rest, feature)), 0.0
        ).astype(jnp.bfloat16)
    head = head_ref[...].astype(jnp.float32)
    for g, frame in enumerate(query_frames(mine, frames)):
        place = place_of(frame, mine, frames)
        lhs_q[g * UROWS : (g + 1) * UROWS, :] = lhs[pl.ds(pl.multiple_of(place * UROWS, 16), UROWS), :]
        gate = time_ref[2, pl.ds(step_ref[frame], 1), :]
        head_g[g * channels : (g + 1) * channels, :] = (head * gate).astype(jnp.bfloat16)
    skip_ref[...] = nt_dot(head_ref[...], patch_ref[...])

    hk_ref[...] = jnp.zeros_like(hk_ref)
    hq_ref[...] = jnp.zeros_like(hq_ref)

    def gained(slot, base, j, rows_ref, count, gain_ref, table_ref, square_ref, keep):
        fetch(slot + j, base, j).wait()
        made = nn_dot(rows_ref[...], wbuf[slot + j])
        made_lo = made.astype(jnp.bfloat16)
        for f in range(count):
            block = made_lo[f * UROWS : (f + 1) * UROWS, :]
            square_ref[f] += nt_dot(block, block)
        if keep:
            table = (made * gain_ref[:, pl.ds(column(j), CHUNK)]).astype(jnp.bfloat16)
            at = pl.multiple_of(j * CHUNK, CHUNK)
            for f in range(count):
                table_ref[f, :, pl.ds(at, CHUNK)] = table[f * UROWS : (f + 1) * UROWS, :]

    def k_step(keep):
        def run(j, carry):
            gained(k_slot, feature, j, lhs, frames, k_gain_ref, ak_ref, hk_ref, keep)
            return carry

        return run

    def q_step(keep):
        def run(j, carry):
            gained(q_slot, 0, j, lhs_q, GROUPS, q_gain_ref, aq_ref, hq_ref, keep)
            return carry

        return run

    def v_step(j, carry):
        fetch(v_slot + j, 2 * feature, j).wait()
        made = nn_dot(lhs[...], wbuf[v_slot + j]).astype(jnp.bfloat16)
        at = pl.multiple_of(j * CHUNK, CHUNK)
        for f in range(frames):
            av_ref[f, :, pl.ds(at, CHUNK)] = made[f * UROWS : (f + 1) * UROWS, :]
        return carry

    lax.fori_loop(0, per_half, k_step(True), 0)
    lax.fori_loop(per_half, whole, k_step(False), 0)
    lax.fori_loop(0, per_half, v_step, 0)
    lax.fori_loop(0, per_half, q_step(True), 0)
    lax.fori_loop(per_half, whole, q_step(False), 0)
    out_copy.wait()
    mixed = nt_dot(head_g[...], obuf[...]).astype(jnp.bfloat16)
    for g in range(GROUPS):
        mix_ref[g] = mixed[g * channels : (g + 1) * channels, :]


def normed_rows(z, gram, square, feature):
    var = jnp.sum(z * nn_dot(gram, z, precision=EXACT), axis=0, keepdims=True)
    scaled = z * lax.rsqrt(var + EPS)
    tail = (UROWS - z.shape[0], z.shape[1])
    ones = (lax.broadcasted_iota(jnp.int32, tail, 0) == 0).astype(jnp.float32)
    rows = jnp.concatenate([scaled, ones], axis=0)
    mean_sq = jnp.sum(rows * nn_dot(square, rows, precision=EXACT), axis=0, keepdims=True) / feature
    return rows, lax.rsqrt(mean_sq + EPS)


def attend_kernel(
    frames,
    feature,
    z_ref,
    ak_ref,
    av_ref,
    aq_ref,
    hk_ref,
    hq_ref,
    gram_ref,
    mix_ref,
    skip_ref,
    part_ref,
    q_s,
    m_s,
    l_s,
    o_s,
):
    mine = lax.axis_index("queue")
    core = mine & 1
    heads = q_s.shape[0]
    tok = z_ref.shape[3]
    blocks = z_ref.shape[0]
    step = min(blocks, 4)
    gram = gram_ref[...]
    scaling = HEAD_DIM ** (-0.5) * math.log2(math.e)
    for g, frame in enumerate(query_frames(mine, frames)):
        z = z_ref[0, place_of(frame, mine, frames)].astype(jnp.float32)
        rows, factor = normed_rows(z, gram, hq_ref[g], feature)
        made = tn_dot((rows * (factor * scaling)).astype(jnp.bfloat16), aq_ref[g]).astype(jnp.bfloat16)
        for h in range(heads):
            q_s[h, g * tok : (g + 1) * tok, :] = made[:, h * HEAD_DIM : (h + 1) * HEAD_DIM]
    m_s[...] = jnp.full_like(m_s, -1e30)
    l_s[...] = jnp.zeros_like(l_s)
    o_s[...] = jnp.zeros_like(o_s)

    def portion(i, carry):
        place = lax.rem(i, frames)
        base = lax.div(i, frames) * step
        z = jnp.concatenate([z_ref[base + b, place] for b in range(step)], axis=1).astype(jnp.float32)
        rows, factor = normed_rows(z, gram, hk_ref[place], feature)
        keys = tn_dot((rows * factor).astype(jnp.bfloat16), ak_ref[place]).astype(jnp.bfloat16)
        values = tn_dot(rows.astype(jnp.bfloat16), av_ref[place]).astype(jnp.bfloat16)
        for h in range(heads):
            span = slice(h * HEAD_DIM, (h + 1) * HEAD_DIM)
            scores = nt_dot(q_s[h], keys[:, span])
            before = m_s[h]
            top = jnp.maximum(before, jnp.max(scores, axis=-1, keepdims=True))
            m_s[h] = top
            alpha = jnp.exp2(before - top)
            weights = jnp.exp2(scores - top[:, :1])
            folded = weights[:, :HEAD_DIM]
            for b in range(1, scores.shape[1] // HEAD_DIM):
                folded = folded + weights[:, b * HEAD_DIM : (b + 1) * HEAD_DIM]
            l_s[h] = l_s[h] * alpha + folded
            o_s[h] = o_s[h] * alpha + nn_dot(weights.astype(jnp.bfloat16), values[:, span])
        return carry

    lax.fori_loop(0, frames * (blocks // step), portion, 0)

    lead = jnp.where(core == 0, 1.0, 0.0)
    totals = []
    for g, frame in enumerate(query_frames(mine, frames)):
        z = z_ref[0, place_of(frame, mine, frames)].astype(jnp.float32)
        totals.append(nn_dot(skip_ref[...], z, precision=EXACT) * lead)
    for h in range(heads):
        done = (o_s[h] / jnp.sum(l_s[h], axis=-1, keepdims=True)).astype(jnp.bfloat16)
        for g in range(GROUPS):
            mix = mix_ref[g, :, h * HEAD_DIM : (h + 1) * HEAD_DIM]
            totals[g] = totals[g] + nt_dot(mix, done[g * tok : (g + 1) * tok, :])
    for g in range(GROUPS):
        part_ref[g] = totals[g]


def swapped(value, axis, bit):
    peers = lax.axis_size(axis)
    return lax.ppermute(value, axis, [(i, i ^ bit) for i in range(peers)])


def per_device(
    latents,
    step_index,
    tail_noise,
    patch_weight,
    time_table,
    qkv_weight,
    q_gain,
    k_gain,
    out_weight,
    head_weight,
):
    channels, feature = patch_weight.shape
    levels = time_table.shape[0]
    frames = lax.axis_size("queue")
    peers = lax.axis_size("tok")
    half = feature // 2
    heads = half // HEAD_DIM
    mine = lax.axis_index("queue")
    latent = latents[0].T
    tok = latent.shape[1]
    f32, bf16 = jnp.float32, jnp.bfloat16

    shapes = (
        ((frames, UROWS, half), bf16),
        ((frames, UROWS, half), bf16),
        ((GROUPS, UROWS, half), bf16),
        ((frames, UROWS, UROWS), f32),
        ((GROUPS, UROWS, UROWS), f32),
        ((channels, channels), f32),
        ((GROUPS, channels, half), bf16),
        ((channels, channels), f32),
    )
    slots = 2 * (feature // CHUNK) + half // CHUNK
    tables = pl.pallas_call(
        functools.partial(tables_kernel, frames),
        out_shape=[jax.ShapeDtypeStruct(*s) for s in shapes],
        in_specs=[SMEM, VMEM, VMEM, ANY, VMEM, VMEM, ANY, VMEM],
        out_specs=[VMEM] * len(shapes),
        scratch_shapes=[
            pltpu.VMEM((frames * UROWS, feature), bf16),
            pltpu.VMEM((GROUPS * UROWS, feature), bf16),
            pltpu.VMEM((GROUPS * channels, feature), bf16),
            pltpu.VMEM((slots, feature, CHUNK), bf16),
            pltpu.VMEM((half, feature), bf16),
            pltpu.SemaphoreType.DMA((slots + 1,)),
        ],
        compiler_params=pltpu.CompilerParams(vmem_limit_bytes=48 << 20),
        cost_estimate=pl.CostEstimate(flops=6 * 10**9, bytes_accessed=18 * 10**6, transcendentals=0),
        name="tables",
    )(
        step_index,
        time_table.transpose(1, 0, 2),
        patch_weight,
        qkv_weight,
        q_gain[None],
        k_gain[None],
        out_weight,
        head_weight.T,
    )

    known = latent.astype(bf16)[None]
    bit = 2
    while bit < frames:
        known = jnp.concatenate([known, swapped(known, "queue", bit)], axis=0)
        bit *= 2
    known = jnp.concatenate([known, swapped(known, "queue", 1)], axis=0)
    gathered = known[None]
    bit = 1
    while bit < peers:
        gathered = jnp.concatenate([gathered, swapped(gathered, "tok", bit)], axis=0)
        bit *= 2

    rows = GROUPS * tok
    part = pl.pallas_call(
        functools.partial(attend_kernel, frames, feature),
        out_shape=jax.ShapeDtypeStruct((GROUPS, channels, tok), f32),
        in_specs=[VMEM] * 9,
        out_specs=VMEM,
        scratch_shapes=[
            pltpu.VMEM((heads, rows, HEAD_DIM), bf16),
            pltpu.VMEM((heads, rows, HEAD_DIM), f32),
            pltpu.VMEM((heads, rows, HEAD_DIM), f32),
            pltpu.VMEM((heads, rows, HEAD_DIM), f32),
        ],
        compiler_params=pltpu.CompilerParams(vmem_limit_bytes=48 << 20),
        cost_estimate=pl.CostEstimate(flops=30 * 10**9, bytes_accessed=8 * 10**6, transcendentals=13 * 10**6),
        name="attend",
    )(gathered, *tables)

    core = mine & 1
    share = channels // frames
    clean = lax.dynamic_slice_in_dim(part[3], share * mine, share, 0)
    clean_other = lax.dynamic_slice_in_dim(part[3], share * (mine ^ 1), share, 0)
    kept = jnp.concatenate([lax.dynamic_slice_in_dim(part, core, 2, 0).reshape(2 * channels, tok), clean], 0)
    given = jnp.concatenate(
        [lax.dynamic_slice_in_dim(part, 1 - core, 2, 0).reshape(2 * channels, tok), clean_other], 0
    )
    total = kept + swapped(given, "queue", 1)
    velocity = total[:channels]

    def drop(frame):
        now = step_index[frame]
        before = jnp.where(frame > 0, step_index[jnp.maximum(frame - 1, 0)], -1)
        return ((before.astype(f32) + 1.0) - (now.astype(f32) + 1.0)) / levels

    following = jnp.minimum(mine + 1, frames - 1)
    there = lax.dynamic_index_in_dim(known, place_of(following, mine, frames), 0, False).astype(f32)
    arrived = there + drop(following) * total[channels : 2 * channels]
    queue_next = jnp.where(mine == frames - 1, tail_noise.T, arrived)
    oldest = lax.dynamic_index_in_dim(known, place_of(0, mine, frames), 0, False).astype(f32)
    oldest = lax.dynamic_slice_in_dim(oldest, share * mine, share, 0)
    leaving = oldest + drop(jnp.int32(0)) * total[2 * channels :]
    return (velocity.T[None], queue_next.T[None], leaving)


def solution(mesh):
    placed = (P("queue", "tok", None), P(), P("tok", None), P(), P(), P(), P(), P(), P(), P())
    return jax.shard_map(
        per_device,
        mesh=mesh,
        in_specs=placed,
        out_specs=(P("queue", "tok", None), P("queue", "tok", None), P("queue", "tok")),
        check_vma=False,
    )
```

```python
import functools
import math

import jax
import jax.numpy as jnp
from jax import lax
from jax.experimental import pallas as pl
from jax.experimental.pallas import tpu as pltpu
from jax.sharding import PartitionSpec as P

HEAD_DIM = 128
EPS = 1e-06
UROWS = 80
GROUPS = 4
CHUNK = 256
EXACT = lax.Precision.HIGHEST
VMEM = pl.BlockSpec(memory_space=pltpu.VMEM)
SMEM = pl.BlockSpec(memory_space=pltpu.SMEM)
ANY = pl.BlockSpec(memory_space=pl.ANY)


def nt_dot(a, b, **kw):
    return lax.dot_general(a, b, (((1,), (1,)), ((), ())), preferred_element_type=jnp.float32, **kw)


def tn_dot(a, b, **kw):
    return lax.dot_general(a, b, (((0,), (0,)), ((), ())), preferred_element_type=jnp.float32, **kw)


def nn_dot(a, b, **kw):
    return jnp.dot(a, b, preferred_element_type=jnp.float32, **kw)


def frame_at(place, mine, frames):
    half = frames // 2
    return mine ^ (((place % half) << 1) | (place // half))


def place_of(frame, mine, frames):
    apart = mine ^ frame
    return (apart >> 1) + (apart & 1) * (frames // 2)


def query_frames(mine, frames):
    first = mine - (mine & 1)
    return (first, first + 1, jnp.minimum(first + 2, frames - 1), 0 * first)


def copies_of(pairs, sems, first):
    made = [pltpu.make_async_copy(src, dst, sems.at[first + i]) for i, (src, dst) in enumerate(pairs)]
    for copy in made:
        copy.start()
    return made


def column(j, half):
    core = lax.axis_index("queue") & 1
    return pl.multiple_of(core * half + j * CHUNK, CHUNK)


def fetches(qkv_ref, wbuf, sems, base, half):
    def fetch(j):
        at = pl.multiple_of(base + column(j, half), CHUNK)
        return pltpu.make_async_copy(qkv_ref.at[:, pl.ds(at, CHUNK)], wbuf.at[j], sems.at[j])

    return fetch


def gained(made, gain, count, j, table_ref, square_ref):
    low = made.astype(jnp.bfloat16)
    for f in range(count):
        block = low[f * UROWS : (f + 1) * UROWS, :]
        square_ref[f] += nt_dot(block, block)
    table = (made * gain).astype(jnp.bfloat16)
    at = pl.multiple_of(j * CHUNK, CHUNK)
    for f in range(count):
        table_ref[f, :, pl.ds(at, CHUNK)] = table[f * UROWS : (f + 1) * UROWS, :]


def key_tables(frames, step_hbm, time_hbm, patch_hbm, qkv_ref, gain_hbm, ak_ref, hk_ref, lhs_ref, gram_ref, step_ref, time_ref, patch_ref, gain_ref, wbuf, sems):
    channels, feature = patch_ref.shape
    half = ak_ref.shape[2]
    mine = lax.axis_index("queue")
    count = half // CHUNK
    fetch = fetches(qkv_ref, wbuf, sems, feature, half)
    at = pl.multiple_of((mine & 1) * half, CHUNK)
    small = copies_of(
        (
            (step_hbm, step_ref),
            (patch_hbm, patch_ref),
            (time_hbm.at[0:2], time_ref),
            (gain_hbm.at[pl.ds(at, half)], gain_ref),
        ),
        sems,
        count,
    )
    for j in range(count):
        fetch(j).start()
    for copy in small:
        copy.wait()
    patch = patch_ref[...].astype(jnp.float32)
    centred = patch - jnp.mean(patch, axis=-1, keepdims=True)
    gram_ref[...] = nt_dot(centred, centred, precision=EXACT) / feature
    rest = UROWS - channels
    first_row = lax.broadcasted_iota(jnp.int32, (rest, feature), 0) == 0
    for place in range(frames):
        level = step_ref[frame_at(place, mine, frames)]
        shift = time_ref[0, pl.ds(level, 1), :]
        scale = time_ref[1, pl.ds(level, 1), :]
        lhs_ref[place * UROWS : place * UROWS + channels, :] = (centred * (1.0 + scale)).astype(jnp.bfloat16)
        lhs_ref[place * UROWS + channels : (place + 1) * UROWS, :] = jnp.where(
            first_row, jnp.broadcast_to(shift, (rest, feature)), 0.0
        ).astype(jnp.bfloat16)
    hk_ref[...] = jnp.zeros_like(hk_ref)

    def run(j, carry):
        fetch(j).wait()
        gain = gain_ref[pl.ds(pl.multiple_of(j * CHUNK, CHUNK), CHUNK)].reshape(1, CHUNK)
        gained(nn_dot(lhs_ref[...], wbuf[j]), gain, frames, j, ak_ref, hk_ref)
        return carry

    lax.fori_loop(0, count, run, 0)


def value_tables(frames, lhs_ref, qkv_ref, av_ref, wbuf, sems):
    feature = lhs_ref.shape[1]
    half = av_ref.shape[2]
    count = half // CHUNK
    fetch = fetches(qkv_ref, wbuf, sems, 2 * feature, half)
    for j in range(count):
        fetch(j).start()

    def run(j, carry):
        fetch(j).wait()
        made = nn_dot(lhs_ref[...], wbuf[j]).astype(jnp.bfloat16)
        at = pl.multiple_of(j * CHUNK, CHUNK)
        for f in range(frames):
            av_ref[f, :, pl.ds(at, CHUNK)] = made[f * UROWS : (f + 1) * UROWS, :]
        return carry

    lax.fori_loop(0, count, run, 0)


def query_tables(frames, step_hbm, time_hbm, patch_hbm, lhs_ref, qkv_ref, gain_hbm, out_hbm, head_hbm, aq_ref, hq_ref, mix_ref, skip_ref, step_ref, time_ref, patch_ref, head_ref, gain_ref, lhs_q, head_g, obuf, wbuf, sems):
    channels, _ = patch_ref.shape
    half = aq_ref.shape[2]
    mine = lax.axis_index("queue")
    count = half // CHUNK
    fetch = fetches(qkv_ref, wbuf, sems, 0, half)
    at = pl.multiple_of((mine & 1) * half, CHUNK)
    small = copies_of(
        (
            (step_hbm, step_ref),
            (gain_hbm.at[pl.ds(at, half)], gain_ref),
            (time_hbm.at[2], time_ref),
            (patch_hbm, patch_ref),
            (head_hbm, head_ref),
        ),
        sems,
        count,
    )
    for j in range(count):
        fetch(j).start()
    out_copy = pltpu.make_async_copy(out_hbm.at[pl.ds(at, half), :], obuf, sems.at[count + len(small)])
    out_copy.start()
    for copy in small:
        copy.wait()
    head = head_ref[...].astype(jnp.float32)
    for g, frame in enumerate(query_frames(mine, frames)):
        place = place_of(frame, mine, frames)
        lhs_q[g * UROWS : (g + 1) * UROWS, :] = lhs_ref[pl.ds(pl.multiple_of(place * UROWS, 16), UROWS), :]
        gate = time_ref[pl.ds(step_ref[frame], 1), :]
        head_g[g * channels : (g + 1) * channels, :] = (head * gate).astype(jnp.bfloat16)
    skip_ref[...] = nt_dot(head_ref[...], patch_ref[...])
    hq_ref[...] = jnp.zeros_like(hq_ref)

    def run(j, carry):
        fetch(j).wait()
        gain = gain_ref[pl.ds(pl.multiple_of(j * CHUNK, CHUNK), CHUNK)].reshape(1, CHUNK)
        gained(nn_dot(lhs_q[...], wbuf[j]), gain, GROUPS, j, aq_ref, hq_ref)
        return carry

    lax.fori_loop(0, count, run, 0)
    out_copy.wait()
    mixed = nt_dot(head_g[...], obuf[...]).astype(jnp.bfloat16)
    for g in range(GROUPS):
        mix_ref[g] = mixed[g * channels : (g + 1) * channels, :]


def split(x):
    high = x.astype(jnp.bfloat16)
    return high, (x - high.astype(jnp.float32)).astype(jnp.bfloat16)


def normed_rows(z, gram, square, feature):
    wide = z.astype(jnp.float32)
    gram_hi, gram_lo = split(gram)
    var = jnp.sum(wide * (nn_dot(gram_hi, z) + nn_dot(gram_lo, z)), axis=0, keepdims=True)
    scaled = wide * lax.rsqrt(var + EPS)
    tail = (UROWS - z.shape[0], z.shape[1])
    ones = (lax.broadcasted_iota(jnp.int32, tail, 0) == 0).astype(jnp.float32)
    rows = jnp.concatenate([scaled, ones], axis=0)
    rows_hi, rows_lo = split(rows)
    square_hi, square_lo = split(square)
    made = nn_dot(square_hi, rows_hi) + nn_dot(square_lo, rows_hi) + nn_dot(square_hi, rows_lo)
    mean_sq = jnp.sum(rows * made, axis=0, keepdims=True) / feature
    return rows, lax.rsqrt(mean_sq + EPS)


def attend_kernel(frames, levels, feature, step_ref, z_ref, far_ref, ak_ref, av_ref, aq_ref, hk_ref, hq_ref, hk_far, hq_far, gram_ref, mix_ref, skip_ref, kept_ref, given_ref, q_s, m_s, o_s, part_s):
    mine = lax.axis_index("queue")
    core = mine & 1
    near = frames // 2
    heads = q_s.shape[0]
    channels, tok = z_ref.shape[2:]
    blocks = z_ref.shape[0]
    step = min(blocks, 4)
    portions = frames * (blocks // step)
    gram = gram_ref[...]
    scaling = HEAD_DIM ** (-0.5) * math.log2(math.e)

    def latent_of(block, frame):
        place = place_of(frame, mine, frames)
        inside = jnp.minimum(place, near - 1)
        outside = jnp.maximum(place - near, 0)
        return jnp.where(
            place < near, z_ref[block, inside].astype(jnp.float32), far_ref[block, outside].astype(jnp.float32)
        )

    for g, frame in enumerate(query_frames(mine, frames)):
        z = latent_of(0, frame).astype(jnp.bfloat16)
        rows, factor = normed_rows(z, gram, hq_ref[g] + hq_far[g], feature)
        made = tn_dot(aq_ref[g], (rows * (factor * scaling)).astype(jnp.bfloat16)).astype(jnp.bfloat16)
        for h in range(heads):
            q_s[h, :, g * tok : (g + 1) * tok] = made[h * HEAD_DIM : (h + 1) * HEAD_DIM, :]

    def portion(safe, source_ref, first, i):
        inside = lax.rem(i, near)
        group = lax.div(i, near)
        place = inside + first
        base = group * step
        z = jnp.concatenate([source_ref[base + b, inside] for b in range(step)], axis=1)
        square = hk_ref[place] + hk_far[inside + near - first]
        rows, factor = normed_rows(z, gram, square, feature)
        key_rows = (rows * factor).T.astype(jnp.bfloat16)
        value_rows = rows.astype(jnp.bfloat16)
        slot = group * frames + place
        at = pl.multiple_of(slot * UROWS, 8)
        asked = [
            nn_dot(ak_ref[place, :, h * HEAD_DIM : (h + 1) * HEAD_DIM], q_s[h]).astype(jnp.bfloat16)
            for h in range(heads)
        ]
        scores = nn_dot(key_rows, asked[0])
        for h in range(heads):
            if safe:
                top = jnp.max(scores, axis=0, keepdims=True)
                m_s[h, pl.ds(slot, 1), :] = top
                scores = scores - top
            weights = jnp.exp2(scores).astype(jnp.bfloat16)
            if h + 1 < heads:
                scores = nn_dot(key_rows, asked[h + 1])
            o_s[h, pl.ds(at, UROWS), :] = nn_dot(value_rows, weights)

    def all_portions(safe):
        for source_ref, first in ((z_ref, 0), (far_ref, near)):

            def run(i, carry, source_ref=source_ref, first=first):
                portion(safe, source_ref, first, i)
                return carry

            lax.fori_loop(0, portions // 2, run, 0)

    all_portions(False)

    def total_weight(h):
        total = o_s[h, channels : channels + 1, :]
        for i in range(1, portions):
            total = total + o_s[h, i * UROWS + channels : i * UROWS + channels + 1, :]
        return total

    flags = jnp.zeros((1, q_s.shape[2]), jnp.float32)
    for h in range(heads):
        total = total_weight(h)
        flags = jnp.maximum(flags, jnp.where((total > 2.0**-60) & (total < 2.0**100), 0.0, 1.0))

    @pl.when(jnp.max(flags) > 0.5)
    def _():
        all_portions(True)

        def rescale(i, carry):
            at = pl.multiple_of(i * UROWS, 8)
            for h in range(heads):
                factor = jnp.exp2(m_s[h, pl.ds(i, 1), :] - jnp.max(m_s[h], axis=0, keepdims=True))
                o_s[h, pl.ds(at, UROWS), :] = o_s[h, pl.ds(at, UROWS), :] * factor
            return carry

        lax.fori_loop(0, portions, rescale, 0)

    lead = jnp.where(core == 0, 1.0, 0.0)
    totals = []
    skip_hi, skip_lo = split(skip_ref[...])
    for frame in query_frames(mine, frames):
        z = latent_of(0, frame).astype(jnp.bfloat16)
        totals.append((nn_dot(skip_hi, z) + nn_dot(skip_lo, z)) * lead)
    for h in range(heads):
        span = slice(h * HEAD_DIM, (h + 1) * HEAD_DIM)
        share = 1.0 / total_weight(h)
        done = jnp.zeros((HEAD_DIM, q_s.shape[2]), jnp.float32)
        for part in range(portions // frames):
            at = slice(part * frames * UROWS, (part + 1) * frames * UROWS)
            mean_rows = (o_s[h, at, :] * share).astype(jnp.bfloat16)
            done = done + tn_dot(av_ref[:, :, span].reshape(frames * UROWS, HEAD_DIM), mean_rows)
        done = done.astype(jnp.bfloat16)
        for g in range(GROUPS):
            totals[g] = totals[g] + nn_dot(mix_ref[g, :, span], done[:, g * tok : (g + 1) * tok])
    for g in range(GROUPS):
        part_s[g] = totals[g]

    def drop(frame):
        before = jnp.where(frame > 0, step_ref[jnp.maximum(frame - 1, 0)], -1)
        return (before.astype(jnp.float32) - step_ref[frame].astype(jnp.float32)) / levels

    lat = channels // frames
    following = jnp.minimum(mine + 1, frames - 1)
    followed = jnp.minimum((mine ^ 1) + 1, frames - 1)
    oldest = latent_of(0, 0 * mine)
    kept_ref[:channels] = part_s[core]
    kept_ref[channels : 2 * channels] = latent_of(0, following) + drop(following) * part_s[core + 1]
    given_ref[:channels] = part_s[1 - core]
    given_ref[channels : 2 * channels] = drop(followed) * part_s[2 - core]
    cleaned = drop(0 * mine) * part_s[GROUPS - 1]
    part_s[0] = cleaned + oldest
    part_s[1] = cleaned
    for i in range(lat):
        kept_ref[2 * channels + i : 2 * channels + i + 1, :] = part_s[0, pl.ds(mine * lat + i, 1), :]
        given_ref[2 * channels + i : 2 * channels + i + 1, :] = part_s[1, pl.ds((mine ^ 1) * lat + i, 1), :]


def finish_kernel(frames, kept_ref, got_ref, tail_ref, velocity_ref, next_ref, leaving_ref):
    channels = velocity_ref.shape[0]
    last = lax.axis_index("queue") == frames - 1
    velocity_ref[...] = kept_ref[:channels] + got_ref[:channels]
    arrived = kept_ref[channels : 2 * channels] + got_ref[channels : 2 * channels]
    next_ref[...] = jnp.where(last, tail_ref[...], arrived)
    leaving_ref[...] = kept_ref[2 * channels :] + got_ref[2 * channels :]


def swapped(value, axis, bit):
    peers = lax.axis_size(axis)
    return lax.ppermute(value, axis, [(i, i ^ bit) for i in range(peers)])


def per_device(
    latents,
    step_index,
    tail_noise,
    patch_weight,
    time_table,
    qkv_weight,
    q_gain,
    k_gain,
    out_weight,
    head_weight,
):
    return one_step(
        latents[0].T,
        step_index,
        tail_noise.T,
        patch_weight,
        time_table.transpose(1, 0, 2),
        qkv_weight,
        q_gain,
        k_gain,
        out_weight,
        head_weight.T,
    )


def shaped(*shapes):
    return [jax.ShapeDtypeStruct(shape, kind) for shape, kind in shapes]


def one_step(latent, step_index, tail, patch, times, qkv, q_gain, k_gain, out_w, head):
    channels, feature = patch.shape
    levels = times.shape[1]
    frames = lax.axis_size("queue")
    peers = lax.axis_size("tok")
    half = feature // 2
    heads = half // HEAD_DIM
    tok = latent.shape[1]
    count = half // CHUNK
    f32, bf16 = jnp.float32, jnp.bfloat16
    params = pltpu.CompilerParams(vmem_limit_bytes=48 << 20)

    ak, hk, lhs, gram = pl.pallas_call(
        functools.partial(key_tables, frames),
        out_shape=shaped(
            ((frames, UROWS, half), bf16),
            ((frames, UROWS, UROWS), f32),
            ((frames * UROWS, feature), bf16),
            ((channels, channels), f32),
        ),
        in_specs=[ANY] * 5,
        out_specs=[VMEM] * 4,
        scratch_shapes=[
            pltpu.SMEM((frames,), jnp.int32),
            pltpu.VMEM((2, levels, feature), f32),
            pltpu.VMEM((channels, feature), bf16),
            pltpu.VMEM((half,), f32),
            pltpu.VMEM((count, feature, CHUNK), bf16),
            pltpu.SemaphoreType.DMA((count + 4,)),
        ],
        compiler_params=params,
        cost_estimate=pl.CostEstimate(flops=2 * 10**9, bytes_accessed=4 * 10**6, transcendentals=0),
        name="key_tables",
    )(step_index, times, patch, qkv, k_gain)
    (av,) = pl.pallas_call(
        functools.partial(value_tables, frames),
        out_shape=shaped(((frames, UROWS, half), bf16)),
        in_specs=[VMEM, ANY],
        out_specs=[VMEM],
        scratch_shapes=[
            pltpu.VMEM((count, feature, CHUNK), bf16),
            pltpu.SemaphoreType.DMA((count,)),
        ],
        compiler_params=params,
        cost_estimate=pl.CostEstimate(flops=2 * 10**9, bytes_accessed=4 * 10**6, transcendentals=0),
        name="value_tables",
    )(lhs, qkv)
    aq, hq, mix, skip = pl.pallas_call(
        functools.partial(query_tables, frames),
        out_shape=shaped(
            ((GROUPS, UROWS, half), bf16),
            ((GROUPS, UROWS, UROWS), f32),
            ((GROUPS, channels, half), bf16),
            ((channels, channels), f32),
        ),
        in_specs=[ANY, ANY, ANY, VMEM, ANY, ANY, ANY, ANY],
        out_specs=[VMEM] * 4,
        scratch_shapes=[
            pltpu.SMEM((frames,), jnp.int32),
            pltpu.VMEM((levels, feature), f32),
            pltpu.VMEM((channels, feature), bf16),
            pltpu.VMEM((channels, feature), bf16),
            pltpu.VMEM((half,), f32),
            pltpu.VMEM((GROUPS * UROWS, feature), bf16),
            pltpu.VMEM((GROUPS * channels, feature), bf16),
            pltpu.VMEM((half, feature), bf16),
            pltpu.VMEM((count, feature, CHUNK), bf16),
            pltpu.SemaphoreType.DMA((count + 6,)),
        ],
        compiler_params=params,
        cost_estimate=pl.CostEstimate(flops=2 * 10**9, bytes_accessed=6 * 10**6, transcendentals=0),
        name="query_tables",
    )(step_index, times, patch, lhs, qkv, q_gain, out_w, head)
    hk_far = swapped(hk, "queue", 1)
    hq_far = swapped(hq, "queue", 1)

    known = latent.astype(bf16)[None]
    bit = 2
    while bit < frames:
        got = swapped(known, "queue", bit)
        known = jnp.concatenate([known, got], axis=0)
        bit *= 2
    known = known[None]
    bit = 1
    while bit < peers:
        got = swapped(known, "tok", bit)
        known = jnp.concatenate([known, got], axis=0)
        bit *= 2
    far = swapped(known, "queue", 1)

    rows = GROUPS * tok
    portions = frames * (peers // min(peers, 4))
    share = channels // frames
    sent = (2 * channels + share, tok)
    kept, given = pl.pallas_call(
        functools.partial(attend_kernel, frames, levels, feature),
        out_shape=shaped((sent, f32), (sent, f32)),
        in_specs=[SMEM] + [VMEM] * 12,
        out_specs=[VMEM] * 2,
        scratch_shapes=[
            pltpu.VMEM((heads, HEAD_DIM, rows), bf16),
            pltpu.VMEM((heads, portions, rows), f32),
            pltpu.VMEM((heads, portions * UROWS, rows), f32),
            pltpu.VMEM((GROUPS, channels, tok), f32),
        ],
        compiler_params=params,
        cost_estimate=pl.CostEstimate(flops=30 * 10**9, bytes_accessed=8 * 10**6, transcendentals=13 * 10**6),
        name="attend",
    )(step_index, known, far, ak, av, aq, hk, hq, hk_far, hq_far, gram, mix, skip)
    got = swapped(given, "queue", 1)
    velocity, queue_next, leaving = pl.pallas_call(
        functools.partial(finish_kernel, frames),
        out_shape=shaped(((channels, tok), f32), ((channels, tok), f32), ((share, tok), f32)),
        in_specs=[VMEM] * 3,
        out_specs=[VMEM] * 3,
        name="finish",
    )(kept, got, tail)
    return (velocity.T[None], queue_next.T[None], leaving)


def solution(mesh):
    placed = (P("queue", "tok", None), P(), P("tok", None), P(), P(), P(), P(), P(), P(), P())
    return jax.shard_map(
        per_device,
        mesh=mesh,
        in_specs=placed,
        out_specs=(P("queue", "tok", None), P("queue", "tok", None), P("queue", "tok")),
        check_vma=False,
    )
```

```python
import functools
import math

import jax
import jax.numpy as jnp
from jax import lax
from jax.experimental import pallas as pl
from jax.experimental.pallas import tpu as pltpu
from jax.sharding import PartitionSpec as P

HEAD_DIM = 128
EPS = 1e-06
UROWS = 80
GROUPS = 4
CHUNK = 256
UNROLL = 2
LIM_TAB = 62500000
EXACT = lax.Precision.HIGHEST
VMEM = pl.BlockSpec(memory_space=pltpu.VMEM)
SMEM = pl.BlockSpec(memory_space=pltpu.SMEM)
HBM = pl.BlockSpec(memory_space=pltpu.HBM)


def nt_dot(a, b, **kw):
    return lax.dot_general(a, b, (((1,), (1,)), ((), ())), preferred_element_type=jnp.float32, **kw)


def tn_dot(a, b, **kw):
    return lax.dot_general(a, b, (((0,), (0,)), ((), ())), preferred_element_type=jnp.float32, **kw)


def nn_dot(a, b, **kw):
    return jnp.dot(a, b, preferred_element_type=jnp.float32, **kw)


def frame_at(place, mine, frames):
    half = frames // 2
    return mine ^ (((place % half) << 1) | (place // half))


def place_of(frame, mine, frames):
    apart = mine ^ frame
    return (apart >> 1) + (apart & 1) * (frames // 2)


def query_frames(mine, frames):
    first = mine - (mine & 1)
    return (first, first + 1, jnp.minimum(first + 2, frames - 1), 0 * first)


def copies_of(pairs, sems, first):
    made = [pltpu.make_async_copy(src, dst, sems.at[first + i]) for i, (src, dst) in enumerate(pairs)]
    for copy in made:
        copy.start()
    return made


def gained(made, gain, first, count, j, table_ref, square_ref):
    low = made.astype(jnp.bfloat16)
    for f in range(count):
        block = low[f * UROWS : (f + 1) * UROWS, :]
        square_ref[first + f] += nt_dot(block, block)
    keep(low if gain is None else (made * gain).astype(jnp.bfloat16), first, count, j, table_ref)


def keep(table, first, count, j, table_ref):
    at = pl.multiple_of(j * CHUNK, CHUNK)
    for f in range(count):
        table_ref[first + f, :, pl.ds(at, CHUNK)] = table[f * UROWS : (f + 1) * UROWS, :]


def centred_patch(patch_ref):
    patch = patch_ref[...].astype(jnp.float32)
    return patch - jnp.mean(patch, axis=-1, keepdims=True)


def fill_rows(lhs, centred, which, step_ref, time_ref):
    channels, feature = centred.shape
    rest = UROWS - channels
    first_row = lax.broadcasted_iota(jnp.int32, (rest, feature), 0) == 0
    for n, frame in enumerate(which):
        level = step_ref[frame]
        shift = time_ref[0, pl.ds(level, 1), :]
        scale = time_ref[1, pl.ds(level, 1), :]
        lhs[n * UROWS : n * UROWS + channels, :] = (centred * (1.0 + scale)).astype(jnp.bfloat16)
        lhs[n * UROWS + channels : (n + 1) * UROWS, :] = jnp.where(
            first_row, jnp.broadcast_to(shift, (rest, feature)), 0.0
        ).astype(jnp.bfloat16)


def tables_kernel(frames, step_hbm, time_hbm, patch_hbm, qkv_hbm, q_gain_hbm, k_gain_hbm, out_hbm, head_hbm, tab_hbm, av_hbm, mix_hbm, sq_ref, step_ref, time_ref, patch_ref, head_ref, q_gain_ref, k_gain_ref, lhs, lhs_q, head_g, tab_ref, av_ref, mix_ref, obuf, wbuf, sems):
    channels, feature = patch_ref.shape
    half = tab_ref.shape[2]
    count = half // CHUNK
    mine = lax.axis_index("queue")
    start = pl.multiple_of((mine & 1) * half, CHUNK)
    small = copies_of(
        (
            (step_hbm, step_ref),
            (patch_hbm, patch_ref),
            (time_hbm, time_ref),
            (head_hbm, head_ref),
            (q_gain_hbm.at[pl.ds(start, half)], q_gain_ref),
            (k_gain_hbm.at[pl.ds(start, half)], k_gain_ref),
        ),
        sems,
        0,
    )
    big = len(small)

    def fetch(part, j):
        base = (feature, 2 * feature, 0)[part]
        at = pl.multiple_of(base + start + j * CHUNK, CHUNK)
        slot = part * count + j
        return pltpu.make_async_copy(qkv_hbm.at[:, pl.ds(at, CHUNK)], wbuf.at[slot], sems.at[big + slot])

    for part in range(3):
        for j in range(count):
            fetch(part, j).start()
    after = big + 3 * count
    out_copy = pltpu.make_async_copy(out_hbm.at[pl.ds(start, half), :], obuf, sems.at[after])
    out_copy.start()
    for copy in small:
        copy.wait()
    centred = centred_patch(patch_ref)
    fill_rows(lhs, centred, [frame_at(p, mine, frames) for p in range(frames)], step_ref, time_ref)
    sq_ref[...] = jnp.zeros_like(sq_ref)
    sq_ref[frames + GROUPS, :channels, :channels] = nt_dot(centred, centred, precision=EXACT) / feature

    def key_step(j, carry):
        fetch(0, j).wait()
        gained(nn_dot(lhs[...], wbuf[j]), None, 0, frames, j, tab_ref, sq_ref)
        return carry

    lax.fori_loop(0, count, key_step, 0)
    done = copies_of(((tab_ref.at[:frames], tab_hbm.at[:frames]),), sems, after + 1)

    def value_step(j, carry):
        fetch(1, j).wait()
        keep(nn_dot(lhs[...], wbuf[count + j]).astype(jnp.bfloat16), 0, frames, j, av_ref)
        return carry

    lax.fori_loop(0, count, value_step, 0)
    done += copies_of(((av_ref, av_hbm),), sems, after + 2)
    which = query_frames(mine, frames)
    head = head_ref[...].astype(jnp.float32)
    for g, frame in enumerate(which):
        place = place_of(frame, mine, frames)
        lhs_q[g * UROWS : (g + 1) * UROWS, :] = lhs[pl.ds(pl.multiple_of(place * UROWS, 16), UROWS), :]
        gate = time_ref[2, pl.ds(step_ref[frame], 1), :]
        head_g[g * channels : (g + 1) * channels, :] = (head * gate).astype(jnp.bfloat16)
    sq_ref[frames + GROUPS + 1, :channels, :channels] = nt_dot(head_ref[...], patch_ref[...])

    def query_step(j, carry):
        fetch(2, j).wait()
        span = pl.ds(pl.multiple_of(j * CHUNK, CHUNK), CHUNK)
        gain = (q_gain_ref[span] * k_gain_ref[span]).reshape(1, CHUNK)
        gained(nn_dot(lhs_q[...], wbuf[2 * count + j]), gain, frames, GROUPS, j, tab_ref, sq_ref)
        return carry

    lax.fori_loop(0, count, query_step, 0)
    done += copies_of(((tab_ref.at[frames:], tab_hbm.at[frames:]),), sems, after + 3)
    out_copy.wait()
    mixed = nt_dot(head_g[...], obuf[...]).astype(jnp.bfloat16)
    for g in range(GROUPS):
        mix_ref[g] = mixed[g * channels : (g + 1) * channels, :]
    done += copies_of(((mix_ref, mix_hbm),), sems, after + 4)
    for copy in done:
        copy.wait()


def split(x):
    high = x.astype(jnp.bfloat16)
    return high, (x - high.astype(jnp.float32)).astype(jnp.bfloat16)


def normed_rows(z, gram, square, feature):
    wide = z.astype(jnp.float32)
    gram_hi, gram_lo = split(gram)
    var = jnp.sum(wide * (nn_dot(gram_hi, z) + nn_dot(gram_lo, z)), axis=0, keepdims=True)
    scaled = wide * lax.rsqrt(jnp.maximum(var, 0.0) + EPS)
    tail = (UROWS - z.shape[0], z.shape[1])
    ones = (lax.broadcasted_iota(jnp.int32, tail, 0) == 0).astype(jnp.float32)
    rows = jnp.concatenate([scaled, ones], axis=0)
    rows_hi, rows_lo = split(rows)
    square_hi, square_lo = split(square)
    made = nn_dot(square_hi, rows_hi) + nn_dot(square_lo, rows_hi) + nn_dot(square_hi, rows_lo)
    mean_sq = jnp.sum(rows * made, axis=0, keepdims=True) / feature
    return rows, lax.rsqrt(jnp.maximum(mean_sq, 0.0) + EPS)


def latent_of(near_ref, far_ref, frame, frames):
    half = frames // 2
    place = place_of(frame, lax.axis_index("queue"), frames)
    inside = near_ref[jnp.minimum(place, half - 1)]
    outside = far_ref[jnp.maximum(place - half, 0)]
    return jnp.where(place < half, inside.astype(jnp.float32), outside.astype(jnp.float32))


def ask_kernel(frames, feature, near_ref, far_ref, tab_ref, sq_ref, sq_far, asked_ref, q_s):
    mine = lax.axis_index("queue")
    heads = q_s.shape[0]
    channels, tok = near_ref.shape[1:]
    gram = sq_ref[frames + GROUPS, :channels, :channels]
    scaling = HEAD_DIM ** (-0.5) * math.log2(math.e)
    for g, frame in enumerate(query_frames(mine, frames)):
        z = latent_of(near_ref, far_ref, frame, frames).astype(jnp.bfloat16)
        rows, factor = normed_rows(z, gram, sq_ref[frames + g] + sq_far[frames + g], feature)
        made = tn_dot(tab_ref[frames + g], (rows * (factor * scaling)).astype(jnp.bfloat16)).astype(jnp.bfloat16)
        for h in range(heads):
            q_s[h, :, g * tok : (g + 1) * tok] = made[h * HEAD_DIM : (h + 1) * HEAD_DIM, :]
    for h in range(heads):
        table = tab_ref[:frames, :, h * HEAD_DIM : (h + 1) * HEAD_DIM].reshape(frames * UROWS, HEAD_DIM)
        asked_ref[h] = nn_dot(table, q_s[h]).astype(jnp.bfloat16)


def each_portion(feature, sources, asked_ref, squares, gram, emit, safe=False):
    heads = asked_ref.shape[0]
    for blocks, first in sources:
        held = blocks[0].shape[0]
        step = min(len(blocks), 4)
        ways = UNROLL if held % UNROLL == 0 else 1
        for group in range(len(blocks) // step):
            used = blocks[group * step : (group + 1) * step]

            def run(i, carry, used=used, first=first, group=group, ways=ways):
                items = []
                for way in range(ways):
                    inside = i * ways + way
                    place = first + inside
                    z = jnp.concatenate([block[inside] for block in used], axis=1)
                    rows, factor = normed_rows(z, gram, squares(place), feature)
                    key_rows = (rows * factor).T.astype(jnp.bfloat16)
                    value_rows = rows.astype(jnp.bfloat16)
                    items += [(h, place, key_rows, value_rows) for h in range(heads)]

                def scores_of(item):
                    h, place, key_rows, _ = item
                    return nn_dot(key_rows, asked_ref[h, rows_at(place), :])

                scores = scores_of(items[0])
                for n, (h, place, unused, value_rows) in enumerate(items):
                    top = None
                    if safe:
                        top = jnp.max(scores, axis=0, keepdims=True)
                        scores = scores - top
                    weights = jnp.exp2(scores).astype(jnp.bfloat16)
                    if n + 1 < len(items):
                        scores = scores_of(items[n + 1])
                    emit(h, place, group, top, nn_dot(value_rows, weights))
                return carry

            lax.fori_loop(0, held // ways, run, 0)


def squares_of(hk_ref, hk_far, frames):
    half = frames // 2
    return lambda place: hk_ref[place] + hk_far[lax.rem(place + half, frames)]


def rows_at(place):
    return pl.ds(pl.multiple_of(place * UROWS, 16), UROWS)


def attend_kernel(frames, levels, feature, step_ref, near_0, near_ref, far_0, far_ref, asked_ref, av_ref, mix_ref, sq_ref, sq_far, kept_ref, given_ref, m_s, o_s, part_s):
    mine = lax.axis_index("queue")
    core = mine & 1
    heads = asked_ref.shape[0]
    blocks, half, channels, tok = near_ref.shape
    gram = sq_ref[frames + GROUPS, :channels, :channels]
    squares = squares_of(sq_ref, sq_far, frames)
    sources = tuple(
        ([own] + [rest.at[b] for b in range(blocks)], first)
        for own, rest, first in ((near_0, near_ref, 0), (far_0, far_ref, half))
    )

    def emit(h, place, group, top, made):
        if group == 0:
            o_s[h, rows_at(place), :] = made
        else:
            o_s[h, rows_at(place), :] += made

    each_portion(feature, sources, asked_ref, squares, gram, emit)

    def total_weight(h):
        total = o_s[h, channels : channels + 1, :]
        for i in range(1, frames):
            total = total + o_s[h, i * UROWS + channels : i * UROWS + channels + 1, :]
        return total

    flags = jnp.zeros((1, o_s.shape[2]), jnp.float32)
    for h in range(heads):
        total = total_weight(h)
        flags = jnp.maximum(flags, jnp.where((total > 2.0**-60) & (total < 2.0**100), 0.0, 1.0))

    @pl.when(jnp.max(flags) > 0.5)
    def _():
        m_s[...] = jnp.full_like(m_s, -1e30)
        o_s[...] = jnp.zeros_like(o_s)

        def shifted(h, place, group, top, made):
            row = pl.ds(place, 1)
            before = m_s[h, row, :]
            after = jnp.maximum(before, top)
            m_s[h, row, :] = after
            o_s[h, rows_at(place), :] = o_s[h, rows_at(place), :] * jnp.exp2(before - after) + made * jnp.exp2(
                top - after
            )

        each_portion(feature, sources, asked_ref, squares, gram, shifted, safe=True)

        def rescale(i, carry):
            for h in range(heads):
                factor = jnp.exp2(m_s[h, pl.ds(i, 1), :] - jnp.max(m_s[h], axis=0, keepdims=True))
                o_s[h, rows_at(i), :] = o_s[h, rows_at(i), :] * factor
            return carry

        lax.fori_loop(0, frames, rescale, 0)

    lead = jnp.where(core == 0, 1.0, 0.0)
    totals = []
    skip_hi, skip_lo = split(sq_ref[frames + GROUPS + 1, :channels, :channels])
    for frame in query_frames(mine, frames):
        z = latent_of(near_0, far_0, frame, frames).astype(jnp.bfloat16)
        totals.append((nn_dot(skip_hi, z) + nn_dot(skip_lo, z)) * lead)
    for h in range(heads):
        span = slice(h * HEAD_DIM, (h + 1) * HEAD_DIM)
        mean_rows = (o_s[h] * (1.0 / total_weight(h))).astype(jnp.bfloat16)
        done = tn_dot(av_ref[:, :, span].reshape(frames * UROWS, HEAD_DIM), mean_rows).astype(jnp.bfloat16)
        for g in range(GROUPS):
            totals[g] = totals[g] + nn_dot(mix_ref[g, :, span], done[:, g * tok : (g + 1) * tok])
    for g in range(GROUPS):
        part_s[g] = totals[g]

    def drop(frame):
        before = jnp.where(frame > 0, step_ref[jnp.maximum(frame - 1, 0)], -1)
        return (before.astype(jnp.float32) - step_ref[frame].astype(jnp.float32)) / levels

    lat = channels // frames
    following = jnp.minimum(mine + 1, frames - 1)
    followed = jnp.minimum((mine ^ 1) + 1, frames - 1)
    kept_ref[:channels] = part_s[core]
    kept_ref[channels : 2 * channels] = (
        latent_of(near_0, far_0, following, frames) + drop(following) * part_s[core + 1]
    )
    given_ref[:channels] = part_s[1 - core]
    given_ref[channels : 2 * channels] = drop(followed) * part_s[2 - core]
    cleaned = drop(0 * mine) * part_s[GROUPS - 1]
    part_s[0] = cleaned + latent_of(near_0, far_0, 0 * mine, frames)
    part_s[1] = cleaned
    for i in range(lat):
        kept_ref[2 * channels + i : 2 * channels + i + 1, :] = part_s[0, pl.ds(mine * lat + i, 1), :]
        given_ref[2 * channels + i : 2 * channels + i + 1, :] = part_s[1, pl.ds((mine ^ 1) * lat + i, 1), :]


def finish_kernel(frames, kept_ref, got_ref, tail_ref, velocity_ref, next_ref, leaving_ref):
    channels = velocity_ref.shape[0]
    last = lax.axis_index("queue") == frames - 1
    velocity_ref[...] = kept_ref[:channels] + got_ref[:channels]
    arrived = kept_ref[channels : 2 * channels] + got_ref[channels : 2 * channels]
    next_ref[...] = jnp.where(last, tail_ref[...], arrived)
    leaving_ref[...] = kept_ref[2 * channels :] + got_ref[2 * channels :]


def swapped(value, axis, bit):
    peers = lax.axis_size(axis)
    return lax.ppermute(value, axis, [(i, i ^ bit) for i in range(peers)])


def per_device(
    latents,
    step_index,
    tail_noise,
    patch_weight,
    time_table,
    qkv_weight,
    q_gain,
    k_gain,
    out_weight,
    head_weight,
):
    return one_step(
        latents[0].T,
        step_index,
        tail_noise.T,
        patch_weight,
        time_table.transpose(1, 0, 2),
        qkv_weight,
        q_gain,
        k_gain,
        out_weight,
        head_weight.T,
    )


def shaped(*shapes):
    return [jax.ShapeDtypeStruct(shape, kind) for shape, kind in shapes]


def one_step(latent, step_index, tail, patch, times, qkv, q_gain, k_gain, out_w, head):
    channels, feature = patch.shape
    levels = times.shape[1]
    frames = lax.axis_size("queue")
    peers = lax.axis_size("tok")
    half = feature // 2
    heads = half // HEAD_DIM
    tok = latent.shape[1]
    count = half // CHUNK
    f32, bf16 = jnp.float32, jnp.bfloat16
    params = pltpu.CompilerParams(vmem_limit_bytes=(24 << 20) * max(1, frames // 8))

    made = (
        ((frames + GROUPS, UROWS, half), bf16),
        ((frames, UROWS, half), bf16),
        ((GROUPS, channels, half), bf16),
    )
    tab, av, mix, sq = pl.pallas_call(
        functools.partial(tables_kernel, frames),
        out_shape=shaped(*made, ((frames + GROUPS + 2, UROWS, UROWS), f32)),
        in_specs=[HBM] * 8,
        out_specs=[HBM] * 3 + [VMEM],
        scratch_shapes=[
            pltpu.SMEM((frames,), jnp.int32),
            pltpu.VMEM((3, levels, feature), f32),
            pltpu.VMEM((channels, feature), bf16),
            pltpu.VMEM((channels, feature), bf16),
            pltpu.VMEM((half,), f32),
            pltpu.VMEM((half,), f32),
            pltpu.VMEM((frames * UROWS, feature), bf16),
            pltpu.VMEM((GROUPS * UROWS, feature), bf16),
            pltpu.VMEM((GROUPS * channels, feature), bf16),
        ]
        + [pltpu.VMEM(*shape) for shape in made]
        + [
            pltpu.VMEM((half, feature), bf16),
            pltpu.VMEM((3 * count, feature, CHUNK), bf16),
            pltpu.SemaphoreType.DMA((3 * count + 11,)),
        ],
        compiler_params=pltpu.CompilerParams(vmem_limit_bytes=LIM_TAB),
        name="tables",
    )(step_index, times, patch, qkv, q_gain, k_gain, out_w, head)
    sq_far = swapped(sq, "queue", 1)

    own = latent.astype(bf16)[None]
    parts = [own]
    for apart in range(2, frames, 2):
        parts.append(swapped(own, "queue", apart))
    known = jnp.concatenate(parts, axis=0)
    own_far = swapped(known, "queue", 1)
    rows = GROUPS * tok
    (asked,) = pl.pallas_call(
        functools.partial(ask_kernel, frames, feature),
        out_shape=shaped(((heads, frames * UROWS, rows), bf16)),
        in_specs=[VMEM] * 5,
        out_specs=[VMEM],
        scratch_shapes=[pltpu.VMEM((heads, HEAD_DIM, rows), bf16)],
        compiler_params=params,
        cost_estimate=pl.CostEstimate(flops=10**9, bytes_accessed=4 * 10**6, transcendentals=0),
        name="ask",
    )(known, own_far, tab, sq, sq_far)

    parts = []
    for apart in range(1, peers):
        parts.append(swapped(known, "tok", apart)[None])
    near = jnp.concatenate(parts, axis=0)
    far = swapped(near, "queue", 1)

    share = channels // frames
    sent = (2 * channels + share, tok)
    kept, given = pl.pallas_call(
        functools.partial(attend_kernel, frames, levels, feature),
        out_shape=shaped((sent, f32), (sent, f32)),
        in_specs=[SMEM] + [VMEM] * 9,
        out_specs=[VMEM] * 2,
        scratch_shapes=[
            pltpu.VMEM((heads, frames, rows), f32),
            pltpu.VMEM((heads, frames * UROWS, rows), f32),
            pltpu.VMEM((GROUPS, channels, tok), f32),
        ],
        compiler_params=params,
        cost_estimate=pl.CostEstimate(flops=8 * 10**9, bytes_accessed=8 * 10**6, transcendentals=6 * 10**6),
        name="attend",
    )(step_index, known, near, own_far, far, asked, av, mix, sq, sq_far)
    got = swapped(given, "queue", 1)
    velocity, queue_next, leaving = pl.pallas_call(
        functools.partial(finish_kernel, frames),
        out_shape=shaped(((channels, tok), f32), ((channels, tok), f32), ((share, tok), f32)),
        in_specs=[VMEM] * 3,
        out_specs=[VMEM] * 3,
        compiler_params=pltpu.CompilerParams(vmem_limit_bytes=4 << 20),
        name="finish",
    )(kept, got, tail)
    return (velocity.T[None], queue_next.T[None], leaving)


def solution(mesh):
    placed = (P("queue", "tok", None), P(), P("tok", None), P(), P(), P(), P(), P(), P(), P())
    return jax.shard_map(
        per_device,
        mesh=mesh,
        in_specs=placed,
        out_specs=(P("queue", "tok", None), P("queue", "tok", None), P("queue", "tok")),
        check_vma=False,
    )
```

```python
import functools
import math

import jax
import jax.numpy as jnp
from jax import lax
from jax.experimental import pallas as pl
from jax.experimental.pallas import tpu as pltpu
from jax.sharding import PartitionSpec as P

HEAD_DIM = 128
EPS = 1e-06
UROWS = 80
GROUPS = 4
CHUNK = 256
UNROLL = 4
PIECES = 2
WIDE = 512
LIM_TAB = 62500000
EXACT = lax.Precision.HIGHEST
VMEM = pl.BlockSpec(memory_space=pltpu.VMEM)
SMEM = pl.BlockSpec(memory_space=pltpu.SMEM)
HBM = pl.BlockSpec(memory_space=pltpu.HBM)


def nt_dot(a, b, **kw):
    return lax.dot_general(a, b, (((1,), (1,)), ((), ())), preferred_element_type=jnp.float32, **kw)


def tn_dot(a, b, **kw):
    return lax.dot_general(a, b, (((0,), (0,)), ((), ())), preferred_element_type=jnp.float32, **kw)


def nn_dot(a, b, **kw):
    return jnp.dot(a, b, preferred_element_type=jnp.float32, **kw)


def frame_at(place, mine, frames):
    half = frames // 2
    return mine ^ (((place % half) << 1) | (place // half))


def place_of(frame, mine, frames):
    apart = mine ^ frame
    return (apart >> 1) + (apart & 1) * (frames // 2)


def query_frames(mine, frames):
    first = mine - (mine & 1)
    return (first, first + 1, jnp.minimum(first + 2, frames - 1), 0 * first)


def copies_of(pairs, sems, first):
    made = [pltpu.make_async_copy(src, dst, sems.at[first + i]) for i, (src, dst) in enumerate(pairs)]
    for copy in made:
        copy.start()
    return made


def span_of(j):
    return pl.ds(pl.multiple_of(j * CHUNK, CHUNK), CHUNK)


def spread_rows(made, count, channels, f):
    shift = made[count * channels + f : count * channels + f + 1, :]
    rest = (UROWS - channels, made.shape[1])
    first = lax.broadcasted_iota(jnp.int32, rest, 0) == 0
    return made[f * channels : (f + 1) * channels, :], jnp.where(first, jnp.broadcast_to(shift, rest), 0.0)


def packed_shifts(rows, feature):
    room = packed(len(rows)) - len(rows)
    if room:
        rows = rows + [jnp.zeros((room, feature), jnp.float32)]
    return jnp.concatenate(rows, axis=0).astype(jnp.bfloat16)


def packed(count):
    return -(-count // 16) * 16


def centred_patch(patch_ref):
    patch = patch_ref[...].astype(jnp.float32)
    return patch - jnp.mean(patch, axis=-1, keepdims=True)


def tables_kernel(frames, step_hbm, time_hbm, patch_hbm, qkv_hbm, q_gain_hbm, k_gain_hbm, out_hbm, head_hbm, tab_hbm, av_hbm, mix_hbm, sq_ref, step_ref, time_ref, patch_ref, head_ref, q_gain_ref, k_gain_ref, lhs, lhs_q, head_g, kv_ref, tab_ref, mix_ref, obuf, wbuf, sems):
    channels, feature = patch_ref.shape
    half = tab_ref.shape[2]
    count = half // CHUNK
    mine = lax.axis_index("queue")
    start = pl.multiple_of((mine & 1) * half, CHUNK)
    small = copies_of(
        (
            (step_hbm, step_ref),
            (patch_hbm, patch_ref),
            (time_hbm, time_ref),
            (head_hbm, head_ref),
            (q_gain_hbm.at[pl.ds(start, half)], q_gain_ref),
            (k_gain_hbm.at[pl.ds(start, half)], k_gain_ref),
        ),
        sems,
        0,
    )
    big = len(small)

    def fetch(part, j):
        base = (feature, 2 * feature, 0)[part]
        at = pl.multiple_of(base + start, CHUNK)
        slot = part * PIECES + j
        rows = pl.ds(j * (feature // PIECES), feature // PIECES)
        return pltpu.make_async_copy(
            qkv_hbm.at[rows, pl.ds(at, half)], wbuf.at[rows, part * half : (part + 1) * half], sems.at[big + slot]
        )

    for part in (0, 1):
        for j in range(PIECES):
            fetch(part, j).start()
    after = big + 3 * PIECES
    out_copy = pltpu.make_async_copy(out_hbm.at[pl.ds(start, half), :], obuf, sems.at[after])
    for copy in small:
        copy.wait()
    centred = centred_patch(patch_ref)
    shifts = []
    for place in range(frames):
        level = step_ref[frame_at(place, mine, frames)]
        shifts.append(time_ref[0, pl.ds(level, 1), :])
        scale = time_ref[1, pl.ds(level, 1), :]
        lhs[place * channels : (place + 1) * channels, :] = (centred * (1.0 + scale)).astype(jnp.bfloat16)
    lhs[frames * channels :, :] = packed_shifts(shifts, feature)
    sq_ref[...] = jnp.zeros_like(sq_ref)
    sq_ref[frames + GROUPS, :channels, :channels] = nt_dot(centred, centred, precision=EXACT) / feature

    for part in (0, 1):
        for j in range(PIECES):
            fetch(part, j).wait()
    for j in range(PIECES):
        fetch(2, j).start()
    out_copy.start()

    def pair_step(j, carry):
        span = pl.ds(pl.multiple_of(j * WIDE, WIDE), WIDE)
        made = nn_dot(lhs[...], wbuf[:, span])
        for f in range(frames):
            top, tail = spread_rows(made, frames, channels, f)
            kv_ref[f, :channels, span] = top.astype(jnp.bfloat16)
            kv_ref[f, channels:, span] = tail.astype(jnp.bfloat16)
        return carry

    lax.fori_loop(0, 2 * half // WIDE, pair_step, 0)
    done = copies_of(
        ((kv_ref.at[:, :, :half], tab_hbm.at[:frames]), (kv_ref.at[:, :, half:], av_hbm)), sems, after + 1
    )
    for f in range(frames):
        block = kv_ref[f, :, :half]
        sq_ref[f] = nt_dot(block, block)
    which = query_frames(mine, frames)
    head = head_ref[...].astype(jnp.float32)
    for g, frame in enumerate(which):
        place = place_of(frame, mine, frames)
        at = pl.ds(pl.multiple_of(place * channels, 16), channels)
        lhs_q[g * channels : (g + 1) * channels, :] = lhs[at, :]
        gate = time_ref[2, pl.ds(step_ref[frame], 1), :]
        head_g[g * channels : (g + 1) * channels, :] = (head * gate).astype(jnp.bfloat16)
    shifts = [time_ref[0, pl.ds(step_ref[frame], 1), :] for frame in which]
    lhs_q[GROUPS * channels :, :] = packed_shifts(shifts, feature)
    sq_ref[frames + GROUPS + 1, :channels, :channels] = nt_dot(head_ref[...], patch_ref[...])

    for j in range(PIECES):
        fetch(2, j).wait()

    def query_step(j, carry):
        gain = (q_gain_ref[span_of(j)] * k_gain_ref[span_of(j)]).reshape(1, CHUNK)
        made = nn_dot(lhs_q[...], wbuf[:, pl.ds(pl.multiple_of(2 * half + j * CHUNK, CHUNK), CHUNK)])
        for g in range(GROUPS):
            both = jnp.concatenate(spread_rows(made, GROUPS, channels, g), axis=0)
            low = both.astype(jnp.bfloat16)
            sq_ref[frames + g] += nt_dot(low, low)
            tab_ref[g, :, span_of(j)] = (both * gain).astype(jnp.bfloat16)
        return carry

    lax.fori_loop(0, count, query_step, 0)
    done += copies_of(((tab_ref, tab_hbm.at[frames:]),), sems, after + 3)
    out_copy.wait()
    mixed = nt_dot(head_g[...], obuf[...]).astype(jnp.bfloat16)
    for g in range(GROUPS):
        mix_ref[g] = mixed[g * channels : (g + 1) * channels, :]
    done += copies_of(((mix_ref, mix_hbm),), sems, after + 4)
    for copy in done:
        copy.wait()


def split(x):
    high = x.astype(jnp.bfloat16)
    return high, (x - high.astype(jnp.float32)).astype(jnp.bfloat16)


def normed_rows(z, gram, square, feature):
    wide = z.astype(jnp.float32)
    gram_hi, gram_lo = split(gram)
    var = jnp.sum(wide * (nn_dot(gram_hi, z) + nn_dot(gram_lo, z)), axis=0, keepdims=True)
    scaled = wide * lax.rsqrt(jnp.maximum(var, 0.0) + EPS)
    tail = (UROWS - z.shape[0], z.shape[1])
    ones = (lax.broadcasted_iota(jnp.int32, tail, 0) == 0).astype(jnp.float32)
    rows = jnp.concatenate([scaled, ones], axis=0)
    rows_hi, rows_lo = split(rows)
    square_hi, square_lo = split(square)
    made = nn_dot(square_hi, rows_hi) + nn_dot(square_lo, rows_hi) + nn_dot(square_hi, rows_lo)
    mean_sq = jnp.sum(rows * made, axis=0, keepdims=True) / feature
    return rows, lax.rsqrt(jnp.maximum(mean_sq, 0.0) + EPS)


def latent_of(near_ref, far_ref, frame, frames):
    half = frames // 2
    place = place_of(frame, lax.axis_index("queue"), frames)
    inside = near_ref[jnp.minimum(place, half - 1)]
    outside = far_ref[jnp.maximum(place - half, 0)]
    return jnp.where(place < half, inside.astype(jnp.float32), outside.astype(jnp.float32))


def ask_kernel(frames, feature, near_ref, far_ref, tab_ref, sq_ref, sq_far, asked_ref, q_s):
    mine = lax.axis_index("queue")
    heads = q_s.shape[0]
    channels, tok = near_ref.shape[1:]
    gram = sq_ref[frames + GROUPS, :channels, :channels]
    scaling = HEAD_DIM ** (-0.5) * math.log2(math.e)
    for g, frame in enumerate(query_frames(mine, frames)):
        z = latent_of(near_ref, far_ref, frame, frames).astype(jnp.bfloat16)
        rows, factor = normed_rows(z, gram, sq_ref[frames + g] + sq_far[frames + g], feature)
        made = tn_dot(tab_ref[frames + g], (rows * (factor * scaling)).astype(jnp.bfloat16)).astype(jnp.bfloat16)
        for h in range(heads):
            q_s[h, :, g * tok : (g + 1) * tok] = made[h * HEAD_DIM : (h + 1) * HEAD_DIM, :]
    for h in range(heads):
        table = tab_ref[:frames, :, h * HEAD_DIM : (h + 1) * HEAD_DIM].reshape(frames * UROWS, HEAD_DIM)
        asked_ref[h] = nn_dot(table, q_s[h]).astype(jnp.bfloat16)


def each_portion(feature, z_s, asked_ref, squares, gram, emit, safe=False):
    heads = asked_ref.shape[0]
    groups, frames = z_s.shape[:2]
    ways = UNROLL if frames % UNROLL == 0 else 1
    for group in range(groups):

        def run(i, carry, group=group):
            items = []
            for way in range(ways):
                place = i * ways + way
                rows, factor = normed_rows(z_s[group, place], gram, squares(place), feature)
                key_rows = (rows * factor).T.astype(jnp.bfloat16)
                value_rows = rows.astype(jnp.bfloat16)
                items += [(h, place, key_rows, value_rows) for h in range(heads)]

            def scores_of(item):
                h, place, key_rows, _ = item
                return nn_dot(key_rows, asked_ref[h, rows_at(place), :])

            scores = scores_of(items[0])
            for n, (h, place, unused, value_rows) in enumerate(items):
                top = None
                if safe:
                    top = jnp.max(scores, axis=0, keepdims=True)
                    scores = scores - top
                weights = jnp.exp2(scores).astype(jnp.bfloat16)
                if n + 1 < len(items):
                    scores = scores_of(items[n + 1])
                emit(h, place, group, top, nn_dot(value_rows, weights))
            return carry

        lax.fori_loop(0, frames // ways, run, 0)


def squares_of(hk_ref, hk_far, frames):
    half = frames // 2
    return lambda place: hk_ref[place] + hk_far[lax.rem(place + half, frames)]


def rows_at(place):
    return pl.ds(pl.multiple_of(place * UROWS, 16), UROWS)


def attend_kernel(frames, levels, feature, step_ref, near_0, near_ref, far_0, far_ref, asked_ref, av_ref, mix_ref, sq_ref, sq_far, kept_ref, given_ref, z_s, m_s, o_s, part_s):
    mine = lax.axis_index("queue")
    core = mine & 1
    heads = asked_ref.shape[0]
    blocks, half, channels, tok = near_ref.shape
    gram = sq_ref[frames + GROUPS, :channels, :channels]
    squares = squares_of(sq_ref, sq_far, frames)
    step = z_s.shape[3] // tok
    for n in range(blocks + 1):
        at = slice((n % step) * tok, (n % step + 1) * tok)
        z_s[n // step, :half, :, at] = near_0[...] if n == 0 else near_ref[n - 1]
        z_s[n // step, half:, :, at] = far_0[...] if n == 0 else far_ref[n - 1]

    def emit(h, place, group, top, made):
        if group == 0:
            o_s[h, rows_at(place), :] = made
        else:
            o_s[h, rows_at(place), :] += made

    each_portion(feature, z_s, asked_ref, squares, gram, emit)

    def total_weight(h):
        total = o_s[h, channels : channels + 1, :]
        for i in range(1, frames):
            total = total + o_s[h, i * UROWS + channels : i * UROWS + channels + 1, :]
        return total

    flags = jnp.zeros((1, o_s.shape[2]), jnp.float32)
    for h in range(heads):
        total = total_weight(h)
        flags = jnp.maximum(flags, jnp.where((total > 2.0**-60) & (total < 2.0**100), 0.0, 1.0))

    @pl.when(jnp.max(flags) > 0.5)
    def _():
        m_s[...] = jnp.full_like(m_s, -1e30)
        o_s[...] = jnp.zeros_like(o_s)

        def shifted(h, place, group, top, made):
            row = pl.ds(place, 1)
            before = m_s[h, row, :]
            after = jnp.maximum(before, top)
            m_s[h, row, :] = after
            o_s[h, rows_at(place), :] = o_s[h, rows_at(place), :] * jnp.exp2(before - after) + made * jnp.exp2(
                top - after
            )

        each_portion(feature, z_s, asked_ref, squares, gram, shifted, safe=True)

        def rescale(i, carry):
            for h in range(heads):
                factor = jnp.exp2(m_s[h, pl.ds(i, 1), :] - jnp.max(m_s[h], axis=0, keepdims=True))
                o_s[h, rows_at(i), :] = o_s[h, rows_at(i), :] * factor
            return carry

        lax.fori_loop(0, frames, rescale, 0)

    lead = jnp.where(core == 0, 1.0, 0.0)
    totals = []
    skip_hi, skip_lo = split(sq_ref[frames + GROUPS + 1, :channels, :channels])
    for frame in query_frames(mine, frames):
        z = latent_of(near_0, far_0, frame, frames).astype(jnp.bfloat16)
        totals.append((nn_dot(skip_hi, z) + nn_dot(skip_lo, z)) * lead)
    for h in range(heads):
        span = slice(h * HEAD_DIM, (h + 1) * HEAD_DIM)
        mean_rows = (o_s[h] * (1.0 / total_weight(h))).astype(jnp.bfloat16)
        done = tn_dot(av_ref[:, :, span].reshape(frames * UROWS, HEAD_DIM), mean_rows).astype(jnp.bfloat16)
        for g in range(GROUPS):
            totals[g] = totals[g] + nn_dot(mix_ref[g, :, span], done[:, g * tok : (g + 1) * tok])
    for g in range(GROUPS):
        part_s[g] = totals[g]

    def drop(frame):
        before = jnp.where(frame > 0, step_ref[jnp.maximum(frame - 1, 0)], -1)
        return (before.astype(jnp.float32) - step_ref[frame].astype(jnp.float32)) / levels

    lat = channels // frames
    following = jnp.minimum(mine + 1, frames - 1)
    followed = jnp.minimum((mine ^ 1) + 1, frames - 1)
    kept_ref[:channels] = part_s[core]
    kept_ref[channels : 2 * channels] = (
        latent_of(near_0, far_0, following, frames) + drop(following) * part_s[core + 1]
    )
    given_ref[:channels] = part_s[1 - core]
    given_ref[channels : 2 * channels] = drop(followed) * part_s[2 - core]
    cleaned = drop(0 * mine) * part_s[GROUPS - 1]
    part_s[0] = cleaned + latent_of(near_0, far_0, 0 * mine, frames)
    part_s[1] = cleaned
    for i in range(lat):
        kept_ref[2 * channels + i : 2 * channels + i + 1, :] = part_s[0, pl.ds(mine * lat + i, 1), :]
        given_ref[2 * channels + i : 2 * channels + i + 1, :] = part_s[1, pl.ds((mine ^ 1) * lat + i, 1), :]


def finish_kernel(frames, kept_ref, got_ref, tail_ref, velocity_ref, next_ref, leaving_ref):
    channels = velocity_ref.shape[0]
    last = lax.axis_index("queue") == frames - 1
    velocity_ref[...] = kept_ref[:channels] + got_ref[:channels]
    arrived = kept_ref[channels : 2 * channels] + got_ref[channels : 2 * channels]
    next_ref[...] = jnp.where(last, tail_ref[...], arrived)
    leaving_ref[...] = kept_ref[2 * channels :] + got_ref[2 * channels :]


def swapped(value, axis, bit):
    peers = lax.axis_size(axis)
    return lax.ppermute(value, axis, [(i, i ^ bit) for i in range(peers)])


def per_device(
    latents,
    step_index,
    tail_noise,
    patch_weight,
    time_table,
    qkv_weight,
    q_gain,
    k_gain,
    out_weight,
    head_weight,
):
    return one_step(
        latents[0].T,
        step_index,
        tail_noise.T,
        patch_weight,
        time_table.transpose(1, 0, 2),
        qkv_weight,
        q_gain,
        k_gain,
        out_weight,
        head_weight.T,
    )


def shaped(*shapes):
    return [jax.ShapeDtypeStruct(shape, kind) for shape, kind in shapes]


def one_step(latent, step_index, tail, patch, times, qkv, q_gain, k_gain, out_w, head):
    channels, feature = patch.shape
    levels = times.shape[1]
    frames = lax.axis_size("queue")
    peers = lax.axis_size("tok")
    half = feature // 2
    heads = half // HEAD_DIM
    tok = latent.shape[1]
    f32, bf16 = jnp.float32, jnp.bfloat16
    params = pltpu.CompilerParams(vmem_limit_bytes=(24 << 20) * max(1, frames // 8))

    made = (
        ((frames + GROUPS, UROWS, half), bf16),
        ((frames, UROWS, half), bf16),
        ((GROUPS, channels, half), bf16),
    )
    tab, av, mix, sq = pl.pallas_call(
        functools.partial(tables_kernel, frames),
        out_shape=shaped(*made, ((frames + GROUPS + 2, UROWS, UROWS), f32)),
        in_specs=[HBM] * 8,
        out_specs=[HBM] * 3 + [VMEM],
        scratch_shapes=[
            pltpu.SMEM((frames,), jnp.int32),
            pltpu.VMEM((3, levels, feature), f32),
            pltpu.VMEM((channels, feature), bf16),
            pltpu.VMEM((channels, feature), bf16),
            pltpu.VMEM((half,), f32),
            pltpu.VMEM((half,), f32),
            pltpu.VMEM((frames * channels + packed(frames), feature), bf16),
            pltpu.VMEM((GROUPS * channels + packed(GROUPS), feature), bf16),
            pltpu.VMEM((GROUPS * channels, feature), bf16),
        ]
        + [
            pltpu.VMEM((frames, UROWS, 2 * half), bf16),
            pltpu.VMEM((GROUPS, UROWS, half), bf16),
            pltpu.VMEM((GROUPS, channels, half), bf16),
            pltpu.VMEM((half, feature), bf16),
            pltpu.VMEM((feature, 3 * half), bf16),
            pltpu.SemaphoreType.DMA((3 * PIECES + 11,)),
        ],
        compiler_params=pltpu.CompilerParams(vmem_limit_bytes=LIM_TAB),
        name="tables",
    )(step_index, times, patch, qkv, q_gain, k_gain, out_w, head)
    sq_far = swapped(sq, "queue", 1)

    own = latent.astype(bf16)[None]
    parts = [own]
    for apart in range(2, frames, 2):
        parts.append(swapped(own, "queue", apart))
    known = jnp.concatenate(parts, axis=0)
    own_far = swapped(known, "queue", 1)
    rows = GROUPS * tok
    (asked,) = pl.pallas_call(
        functools.partial(ask_kernel, frames, feature),
        out_shape=shaped(((heads, frames * UROWS, rows), bf16)),
        in_specs=[VMEM] * 5,
        out_specs=[VMEM],
        scratch_shapes=[pltpu.VMEM((heads, HEAD_DIM, rows), bf16)],
        compiler_params=params,
        cost_estimate=pl.CostEstimate(flops=10**9, bytes_accessed=4 * 10**6, transcendentals=0),
        name="ask",
    )(known, own_far, tab, sq, sq_far)

    parts = []
    for apart in range(1, peers):
        parts.append(swapped(known, "tok", apart)[None])
    near = jnp.concatenate(parts, axis=0)
    far = swapped(near, "queue", 1)

    held = min(peers, 4)
    share = channels // frames
    sent = (2 * channels + share, tok)
    kept, given = pl.pallas_call(
        functools.partial(attend_kernel, frames, levels, feature),
        out_shape=shaped((sent, f32), (sent, f32)),
        in_specs=[SMEM] + [VMEM] * 9,
        out_specs=[VMEM] * 2,
        scratch_shapes=[
            pltpu.VMEM((peers // held, frames, channels, held * tok), bf16),
            pltpu.VMEM((heads, frames, rows), f32),
            pltpu.VMEM((heads, frames * UROWS, rows), f32),
            pltpu.VMEM((GROUPS, channels, tok), f32),
        ],
        compiler_params=params,
        cost_estimate=pl.CostEstimate(flops=8 * 10**9, bytes_accessed=8 * 10**6, transcendentals=6 * 10**6),
        name="attend",
    )(step_index, known, near, own_far, far, asked, av, mix, sq, sq_far)
    got = swapped(given, "queue", 1)
    velocity, queue_next, leaving = pl.pallas_call(
        functools.partial(finish_kernel, frames),
        out_shape=shaped(((channels, tok), f32), ((channels, tok), f32), ((share, tok), f32)),
        in_specs=[VMEM] * 3,
        out_specs=[VMEM] * 3,
        compiler_params=pltpu.CompilerParams(vmem_limit_bytes=4 << 20),
        name="finish",
    )(kept, got, tail)
    return (velocity.T[None], queue_next.T[None], leaving)


def solution(mesh):
    placed = (P("queue", "tok", None), P(), P("tok", None), P(), P(), P(), P(), P(), P(), P())
    return jax.shard_map(
        per_device,
        mesh=mesh,
        in_specs=placed,
        out_specs=(P("queue", "tok", None), P("queue", "tok", None), P("queue", "tok")),
        check_vma=False,
    )
```

```python
import functools
import math

import jax
import jax.numpy as jnp
from jax import lax
from jax.experimental import pallas as pl
from jax.experimental.pallas import tpu as pltpu
from jax.sharding import PartitionSpec as P

HEAD_DIM = 128
EPS = 1e-06
UROWS = 80
GROUPS = 4
CHUNK = 256
UNROLL = 4
WIDE = 512
LIM_TAB = 62500000
EXACT = lax.Precision.HIGHEST
VMEM = pl.BlockSpec(memory_space=pltpu.VMEM)
SMEM = pl.BlockSpec(memory_space=pltpu.SMEM)
HBM = pl.BlockSpec(memory_space=pltpu.HBM)


def nt_dot(a, b, **kw):
    return lax.dot_general(a, b, (((1,), (1,)), ((), ())), preferred_element_type=jnp.float32, **kw)


def tn_dot(a, b, **kw):
    return lax.dot_general(a, b, (((0,), (0,)), ((), ())), preferred_element_type=jnp.float32, **kw)


def nn_dot(a, b, **kw):
    return jnp.dot(a, b, preferred_element_type=jnp.float32, **kw)


def frame_at(place, mine, frames):
    half = frames // 2
    return mine ^ (((place % half) << 1) | (place // half))


def place_of(frame, mine, frames):
    apart = mine ^ frame
    return (apart >> 1) + (apart & 1) * (frames // 2)


def query_frames(mine, frames):
    first = mine - (mine & 1)
    return (first, first + 1, jnp.minimum(first + 2, frames - 1), 0 * first)


def copies_of(pairs, sems, first):
    made = [pltpu.make_async_copy(src, dst, sems.at[first + i]) for i, (src, dst) in enumerate(pairs)]
    for copy in made:
        copy.start()
    return made


def span_of(j):
    return pl.ds(pl.multiple_of(j * CHUNK, CHUNK), CHUNK)


def spread_rows(made, count, channels, f):
    shift = made[count * channels + f : count * channels + f + 1, :]
    rest = (UROWS - channels, made.shape[1])
    first = lax.broadcasted_iota(jnp.int32, rest, 0) == 0
    return made[f * channels : (f + 1) * channels, :], jnp.where(first, jnp.broadcast_to(shift, rest), 0.0)


def packed_shifts(rows, feature):
    room = packed(len(rows)) - len(rows)
    if room:
        rows = rows + [jnp.zeros((room, feature), jnp.float32)]
    return jnp.concatenate(rows, axis=0).astype(jnp.bfloat16)


def packed(count):
    return -(-count // 16) * 16


def centred_patch(patch_ref):
    patch = patch_ref[...].astype(jnp.float32)
    return patch - jnp.mean(patch, axis=-1, keepdims=True)


def tables_kernel(frames, step_hbm, time_hbm, patch_hbm, qkv_hbm, q_gain_hbm, k_gain_hbm, out_hbm, head_hbm, tab_hbm, av_hbm, mix_hbm, sq_ref, step_ref, time_ref, patch_ref, head_ref, q_gain_ref, k_gain_ref, lhs, lhs_q, head_g, kv_ref, tab_ref, mix_ref, obuf, wbuf, sems):
    channels, feature = patch_ref.shape
    half = tab_ref.shape[2]
    count = half // CHUNK
    mine = lax.axis_index("queue")
    start = pl.multiple_of((mine & 1) * half, CHUNK)
    small = copies_of(
        (
            (step_hbm, step_ref),
            (patch_hbm, patch_ref),
            (time_hbm, time_ref),
            (head_hbm, head_ref),
            (q_gain_hbm.at[pl.ds(start, half)], q_gain_ref),
            (k_gain_hbm.at[pl.ds(start, half)], k_gain_ref),
        ),
        sems,
        0,
    )
    big = len(small)

    def fetch(n):
        base = jnp.where(n < count, feature, jnp.where(n < 2 * count, 2 * feature - half, -2 * half))
        at = pl.multiple_of(base + start + n * CHUNK, CHUNK)
        return pltpu.make_async_copy(
            qkv_hbm.at[:, pl.ds(at, CHUNK)], wbuf.at[:, span_of(n)], sems.at[big + n]
        )

    for n in range(2 * count):
        fetch(n).start()
    after = big + 3 * count
    out_copy = pltpu.make_async_copy(out_hbm.at[pl.ds(start, half), :], obuf, sems.at[after])
    for copy in small:
        copy.wait()
    centred = centred_patch(patch_ref)
    shifts = []
    for place in range(frames):
        level = step_ref[frame_at(place, mine, frames)]
        shifts.append(time_ref[0, pl.ds(level, 1), :])
        scale = time_ref[1, pl.ds(level, 1), :]
        lhs[place * channels : (place + 1) * channels, :] = (centred * (1.0 + scale)).astype(jnp.bfloat16)
    lhs[frames * channels :, :] = packed_shifts(shifts, feature)
    sq_ref[...] = jnp.zeros_like(sq_ref)
    sq_ref[frames + GROUPS, :channels, :channels] = nt_dot(centred, centred, precision=EXACT) / feature

    ratio = WIDE // CHUNK
    for n in range(ratio):
        fetch(n).wait()
    for n in range(2 * count, 3 * count):
        fetch(n).start()
    out_copy.start()

    def pair_step(j, carry):
        @pl.when(j > 0)
        def _():
            for n in range(ratio):
                fetch(j * ratio + n).wait()

        span = pl.ds(pl.multiple_of(j * WIDE, WIDE), WIDE)
        made = nn_dot(lhs[...], wbuf[:, span])
        for f in range(frames):
            top, tail = spread_rows(made, frames, channels, f)
            kv_ref[f, :channels, span] = top.astype(jnp.bfloat16)
            kv_ref[f, channels:, span] = tail.astype(jnp.bfloat16)
        return carry

    lax.fori_loop(0, 2 * half // WIDE, pair_step, 0)
    done = copies_of(
        ((kv_ref.at[:, :, :half], tab_hbm.at[:frames]), (kv_ref.at[:, :, half:], av_hbm)), sems, after + 1
    )
    for f in range(frames):
        block = kv_ref[f, :, :half]
        sq_ref[f] = nt_dot(block, block)
    which = query_frames(mine, frames)
    head = head_ref[...].astype(jnp.float32)
    for g, frame in enumerate(which):
        place = place_of(frame, mine, frames)
        at = pl.ds(pl.multiple_of(place * channels, 16), channels)
        lhs_q[g * channels : (g + 1) * channels, :] = lhs[at, :]
        gate = time_ref[2, pl.ds(step_ref[frame], 1), :]
        head_g[g * channels : (g + 1) * channels, :] = (head * gate).astype(jnp.bfloat16)
    shifts = [time_ref[0, pl.ds(step_ref[frame], 1), :] for frame in which]
    lhs_q[GROUPS * channels :, :] = packed_shifts(shifts, feature)
    sq_ref[frames + GROUPS + 1, :channels, :channels] = nt_dot(head_ref[...], patch_ref[...])


    def query_step(j, carry):
        fetch(2 * count + j).wait()
        gain = (q_gain_ref[span_of(j)] * k_gain_ref[span_of(j)]).reshape(1, CHUNK)
        made = nn_dot(lhs_q[...], wbuf[:, pl.ds(pl.multiple_of(2 * half + j * CHUNK, CHUNK), CHUNK)])
        for g in range(GROUPS):
            both = jnp.concatenate(spread_rows(made, GROUPS, channels, g), axis=0)
            low = both.astype(jnp.bfloat16)
            sq_ref[frames + g] += nt_dot(low, low)
            tab_ref[g, :, span_of(j)] = (both * gain).astype(jnp.bfloat16)
        return carry

    lax.fori_loop(0, count, query_step, 0)
    done += copies_of(((tab_ref, tab_hbm.at[frames:]),), sems, after + 3)
    out_copy.wait()
    mixed = nt_dot(head_g[...], obuf[...]).astype(jnp.bfloat16)
    for g in range(GROUPS):
        mix_ref[g] = mixed[g * channels : (g + 1) * channels, :]
    done += copies_of(((mix_ref, mix_hbm),), sems, after + 4)
    for copy in done:
        copy.wait()


def split(x):
    high = x.astype(jnp.bfloat16)
    return high, (x - high.astype(jnp.float32)).astype(jnp.bfloat16)


def normed_rows(z, gram, square, feature):
    wide = z.astype(jnp.float32)
    gram_hi, gram_lo = split(gram)
    var = jnp.sum(wide * (nn_dot(gram_hi, z) + nn_dot(gram_lo, z)), axis=0, keepdims=True)
    scaled = wide * lax.rsqrt(jnp.maximum(var, 0.0) + EPS)
    tail = (UROWS - z.shape[0], z.shape[1])
    ones = (lax.broadcasted_iota(jnp.int32, tail, 0) == 0).astype(jnp.float32)
    rows = jnp.concatenate([scaled, ones], axis=0)
    rows_hi, rows_lo = split(rows)
    square_hi, square_lo = split(square)
    made = nn_dot(square_hi, rows_hi) + nn_dot(square_lo, rows_hi) + nn_dot(square_hi, rows_lo)
    mean_sq = jnp.sum(rows * made, axis=0, keepdims=True) / feature
    return rows, lax.rsqrt(jnp.maximum(mean_sq, 0.0) + EPS)


def latent_of(near_ref, far_ref, frame, frames):
    half = frames // 2
    place = place_of(frame, lax.axis_index("queue"), frames)
    inside = near_ref[jnp.minimum(place, half - 1)]
    outside = far_ref[jnp.maximum(place - half, 0)]
    return jnp.where(place < half, inside.astype(jnp.float32), outside.astype(jnp.float32))


def ask_kernel(frames, feature, near_ref, far_ref, tab_ref, sq_ref, sq_far, asked_ref, q_s):
    mine = lax.axis_index("queue")
    heads = q_s.shape[0]
    channels, tok = near_ref.shape[1:]
    gram = sq_ref[frames + GROUPS, :channels, :channels]
    scaling = HEAD_DIM ** (-0.5) * math.log2(math.e)
    for g, frame in enumerate(query_frames(mine, frames)):
        z = latent_of(near_ref, far_ref, frame, frames).astype(jnp.bfloat16)
        rows, factor = normed_rows(z, gram, sq_ref[frames + g] + sq_far[frames + g], feature)
        made = tn_dot(tab_ref[frames + g], (rows * (factor * scaling)).astype(jnp.bfloat16)).astype(jnp.bfloat16)
        for h in range(heads):
            q_s[h, :, g * tok : (g + 1) * tok] = made[h * HEAD_DIM : (h + 1) * HEAD_DIM, :]
    for h in range(heads):
        table = tab_ref[:frames, :, h * HEAD_DIM : (h + 1) * HEAD_DIM].reshape(frames * UROWS, HEAD_DIM)
        asked_ref[h] = nn_dot(table, q_s[h]).astype(jnp.bfloat16)


def each_portion(feature, z_s, asked_ref, squares, gram, emit, safe=False):
    heads = asked_ref.shape[0]
    groups, frames = z_s.shape[:2]
    ways = UNROLL if frames % UNROLL == 0 else 1
    for group in range(groups):

        def run(i, carry, group=group):
            items = []
            for way in range(ways):
                place = i * ways + way
                rows, factor = normed_rows(z_s[group, place], gram, squares(place), feature)
                key_rows = (rows * factor).T.astype(jnp.bfloat16)
                value_rows = rows.astype(jnp.bfloat16)
                items += [(h, place, key_rows, value_rows) for h in range(heads)]

            def scores_of(item):
                h, place, key_rows, _ = item
                return nn_dot(key_rows, asked_ref[h, rows_at(place), :])

            scores = scores_of(items[0])
            for n, (h, place, unused, value_rows) in enumerate(items):
                top = None
                if safe:
                    top = jnp.max(scores, axis=0, keepdims=True)
                    scores = scores - top
                weights = jnp.exp2(scores).astype(jnp.bfloat16)
                if n + 1 < len(items):
                    scores = scores_of(items[n + 1])
                emit(h, place, group, top, nn_dot(value_rows, weights))
            return carry

        lax.fori_loop(0, frames // ways, run, 0)


def squares_of(hk_ref, hk_far, frames):
    half = frames // 2
    return lambda place: hk_ref[place] + hk_far[lax.rem(place + half, frames)]


def rows_at(place):
    return pl.ds(pl.multiple_of(place * UROWS, 16), UROWS)


def attend_kernel(frames, levels, feature, step_ref, near_0, near_ref, far_0, far_ref, asked_ref, av_ref, mix_ref, sq_ref, sq_far, kept_ref, given_ref, z_s, m_s, o_s, part_s):
    mine = lax.axis_index("queue")
    core = mine & 1
    heads = asked_ref.shape[0]
    blocks, half, channels, tok = near_ref.shape
    gram = sq_ref[frames + GROUPS, :channels, :channels]
    squares = squares_of(sq_ref, sq_far, frames)
    step = z_s.shape[3] // tok
    for n in range(blocks + 1):
        at = slice((n % step) * tok, (n % step + 1) * tok)
        z_s[n // step, :half, :, at] = near_0[...] if n == 0 else near_ref[n - 1]
        z_s[n // step, half:, :, at] = far_0[...] if n == 0 else far_ref[n - 1]

    def emit(h, place, group, top, made):
        if group == 0:
            o_s[h, rows_at(place), :] = made
        else:
            o_s[h, rows_at(place), :] += made

    each_portion(feature, z_s, asked_ref, squares, gram, emit)

    def total_weight(h):
        total = o_s[h, channels : channels + 1, :]
        for i in range(1, frames):
            total = total + o_s[h, i * UROWS + channels : i * UROWS + channels + 1, :]
        return total

    flags = jnp.zeros((1, o_s.shape[2]), jnp.float32)
    for h in range(heads):
        total = total_weight(h)
        flags = jnp.maximum(flags, jnp.where((total > 2.0**-60) & (total < 2.0**100), 0.0, 1.0))

    @pl.when(jnp.max(flags) > 0.5)
    def _():
        m_s[...] = jnp.full_like(m_s, -1e30)
        o_s[...] = jnp.zeros_like(o_s)

        def shifted(h, place, group, top, made):
            row = pl.ds(place, 1)
            before = m_s[h, row, :]
            after = jnp.maximum(before, top)
            m_s[h, row, :] = after
            o_s[h, rows_at(place), :] = o_s[h, rows_at(place), :] * jnp.exp2(before - after) + made * jnp.exp2(
                top - after
            )

        each_portion(feature, z_s, asked_ref, squares, gram, shifted, safe=True)

        def rescale(i, carry):
            for h in range(heads):
                factor = jnp.exp2(m_s[h, pl.ds(i, 1), :] - jnp.max(m_s[h], axis=0, keepdims=True))
                o_s[h, rows_at(i), :] = o_s[h, rows_at(i), :] * factor
            return carry

        lax.fori_loop(0, frames, rescale, 0)

    lead = jnp.where(core == 0, 1.0, 0.0)
    totals = []
    skip_hi, skip_lo = split(sq_ref[frames + GROUPS + 1, :channels, :channels])
    for frame in query_frames(mine, frames):
        z = latent_of(near_0, far_0, frame, frames).astype(jnp.bfloat16)
        totals.append((nn_dot(skip_hi, z) + nn_dot(skip_lo, z)) * lead)
    for h in range(heads):
        span = slice(h * HEAD_DIM, (h + 1) * HEAD_DIM)
        mean_rows = (o_s[h] * (1.0 / total_weight(h))).astype(jnp.bfloat16)
        done = tn_dot(av_ref[:, :, span].reshape(frames * UROWS, HEAD_DIM), mean_rows).astype(jnp.bfloat16)
        for g in range(GROUPS):
            totals[g] = totals[g] + nn_dot(mix_ref[g, :, span], done[:, g * tok : (g + 1) * tok])
    for g in range(GROUPS):
        part_s[g] = totals[g]

    def drop(frame):
        before = jnp.where(frame > 0, step_ref[jnp.maximum(frame - 1, 0)], -1)
        return (before.astype(jnp.float32) - step_ref[frame].astype(jnp.float32)) / levels

    lat = channels // frames
    following = jnp.minimum(mine + 1, frames - 1)
    followed = jnp.minimum((mine ^ 1) + 1, frames - 1)
    kept_ref[:channels] = part_s[core]
    kept_ref[channels : 2 * channels] = (
        latent_of(near_0, far_0, following, frames) + drop(following) * part_s[core + 1]
    )
    given_ref[:channels] = part_s[1 - core]
    given_ref[channels : 2 * channels] = drop(followed) * part_s[2 - core]
    cleaned = drop(0 * mine) * part_s[GROUPS - 1]
    part_s[0] = cleaned + latent_of(near_0, far_0, 0 * mine, frames)
    part_s[1] = cleaned
    for i in range(lat):
        kept_ref[2 * channels + i : 2 * channels + i + 1, :] = part_s[0, pl.ds(mine * lat + i, 1), :]
        given_ref[2 * channels + i : 2 * channels + i + 1, :] = part_s[1, pl.ds((mine ^ 1) * lat + i, 1), :]


def finish_kernel(frames, kept_ref, got_ref, tail_ref, velocity_ref, next_ref, leaving_ref):
    channels = velocity_ref.shape[0]
    last = lax.axis_index("queue") == frames - 1
    velocity_ref[...] = kept_ref[:channels] + got_ref[:channels]
    arrived = kept_ref[channels : 2 * channels] + got_ref[channels : 2 * channels]
    next_ref[...] = jnp.where(last, tail_ref[...], arrived)
    leaving_ref[...] = kept_ref[2 * channels :] + got_ref[2 * channels :]


def swapped(value, axis, bit):
    peers = lax.axis_size(axis)
    return lax.ppermute(value, axis, [(i, i ^ bit) for i in range(peers)])


def per_device(
    latents,
    step_index,
    tail_noise,
    patch_weight,
    time_table,
    qkv_weight,
    q_gain,
    k_gain,
    out_weight,
    head_weight,
):
    return one_step(
        latents[0].T,
        step_index,
        tail_noise.T,
        patch_weight,
        time_table.transpose(1, 0, 2),
        qkv_weight,
        q_gain,
        k_gain,
        out_weight,
        head_weight.T,
    )


def shaped(*shapes):
    return [jax.ShapeDtypeStruct(shape, kind) for shape, kind in shapes]


def one_step(latent, step_index, tail, patch, times, qkv, q_gain, k_gain, out_w, head):
    channels, feature = patch.shape
    levels = times.shape[1]
    frames = lax.axis_size("queue")
    peers = lax.axis_size("tok")
    half = feature // 2
    heads = half // HEAD_DIM
    tok = latent.shape[1]
    count = half // CHUNK
    f32, bf16 = jnp.float32, jnp.bfloat16
    params = pltpu.CompilerParams(vmem_limit_bytes=(24 << 20) * max(1, frames // 8))

    made = (
        ((frames + GROUPS, UROWS, half), bf16),
        ((frames, UROWS, half), bf16),
        ((GROUPS, channels, half), bf16),
    )
    tab, av, mix, sq = pl.pallas_call(
        functools.partial(tables_kernel, frames),
        out_shape=shaped(*made, ((frames + GROUPS + 2, UROWS, UROWS), f32)),
        in_specs=[HBM] * 8,
        out_specs=[HBM] * 3 + [VMEM],
        scratch_shapes=[
            pltpu.SMEM((frames,), jnp.int32),
            pltpu.VMEM((3, levels, feature), f32),
            pltpu.VMEM((channels, feature), bf16),
            pltpu.VMEM((channels, feature), bf16),
            pltpu.VMEM((half,), f32),
            pltpu.VMEM((half,), f32),
            pltpu.VMEM((frames * channels + packed(frames), feature), bf16),
            pltpu.VMEM((GROUPS * channels + packed(GROUPS), feature), bf16),
            pltpu.VMEM((GROUPS * channels, feature), bf16),
        ]
        + [
            pltpu.VMEM((frames, UROWS, 2 * half), bf16),
            pltpu.VMEM((GROUPS, UROWS, half), bf16),
            pltpu.VMEM((GROUPS, channels, half), bf16),
            pltpu.VMEM((half, feature), bf16),
            pltpu.VMEM((feature, 3 * half), bf16),
            pltpu.SemaphoreType.DMA((3 * count + 11,)),
        ],
        compiler_params=pltpu.CompilerParams(vmem_limit_bytes=LIM_TAB),
        name="tables",
    )(step_index, times, patch, qkv, q_gain, k_gain, out_w, head)
    sq_far = swapped(sq, "queue", 1)

    own = latent.astype(bf16)[None]
    parts = [own]
    for apart in range(2, frames, 2):
        parts.append(swapped(own, "queue", apart))
    known = jnp.concatenate(parts, axis=0)
    own_far = swapped(known, "queue", 1)
    rows = GROUPS * tok
    (asked,) = pl.pallas_call(
        functools.partial(ask_kernel, frames, feature),
        out_shape=shaped(((heads, frames * UROWS, rows), bf16)),
        in_specs=[VMEM] * 5,
        out_specs=[VMEM],
        scratch_shapes=[pltpu.VMEM((heads, HEAD_DIM, rows), bf16)],
        compiler_params=params,
        cost_estimate=pl.CostEstimate(flops=10**9, bytes_accessed=4 * 10**6, transcendentals=0),
        name="ask",
    )(known, own_far, tab, sq, sq_far)

    parts = []
    for apart in range(1, peers):
        parts.append(swapped(known, "tok", apart)[None])
    near = jnp.concatenate(parts, axis=0)
    far = swapped(near, "queue", 1)

    held = min(peers, 4)
    share = channels // frames
    sent = (2 * channels + share, tok)
    kept, given = pl.pallas_call(
        functools.partial(attend_kernel, frames, levels, feature),
        out_shape=shaped((sent, f32), (sent, f32)),
        in_specs=[SMEM] + [VMEM] * 9,
        out_specs=[VMEM] * 2,
        scratch_shapes=[
            pltpu.VMEM((peers // held, frames, channels, held * tok), bf16),
            pltpu.VMEM((heads, frames, rows), f32),
            pltpu.VMEM((heads, frames * UROWS, rows), f32),
            pltpu.VMEM((GROUPS, channels, tok), f32),
        ],
        compiler_params=params,
        cost_estimate=pl.CostEstimate(flops=8 * 10**9, bytes_accessed=8 * 10**6, transcendentals=6 * 10**6),
        name="attend",
    )(step_index, known, near, own_far, far, asked, av, mix, sq, sq_far)
    got = swapped(given, "queue", 1)
    velocity, queue_next, leaving = pl.pallas_call(
        functools.partial(finish_kernel, frames),
        out_shape=shaped(((channels, tok), f32), ((channels, tok), f32), ((share, tok), f32)),
        in_specs=[VMEM] * 3,
        out_specs=[VMEM] * 3,
        compiler_params=pltpu.CompilerParams(vmem_limit_bytes=4 << 20),
        name="finish",
    )(kept, got, tail)
    return (velocity.T[None], queue_next.T[None], leaving)


def solution(mesh):
    placed = (P("queue", "tok", None), P(), P("tok", None), P(), P(), P(), P(), P(), P(), P())
    return jax.shard_map(
        per_device,
        mesh=mesh,
        in_specs=placed,
        out_specs=(P("queue", "tok", None), P("queue", "tok", None), P("queue", "tok")),
        check_vma=False,
    )
```

```python
import functools
import math

import jax
import jax.numpy as jnp
from jax import lax
from jax.experimental import pallas as pl
from jax.experimental.pallas import tpu as pltpu
from jax.sharding import PartitionSpec as P

HEAD_DIM = 128
EPS = 1e-06
UROWS = 80
GROUPS = 4
CHUNK = 256
UNROLL = 4
WIDE = 768
LIM_TAB = 62500000
VMEM = pl.BlockSpec(memory_space=pltpu.VMEM)
SMEM = pl.BlockSpec(memory_space=pltpu.SMEM)
HBM = pl.BlockSpec(memory_space=pltpu.HBM)


def nt_dot(a, b, **kw):
    return lax.dot_general(a, b, (((1,), (1,)), ((), ())), preferred_element_type=jnp.float32, **kw)


def tn_dot(a, b, **kw):
    return lax.dot_general(a, b, (((0,), (0,)), ((), ())), preferred_element_type=jnp.float32, **kw)


def nn_dot(a, b, **kw):
    return jnp.dot(a, b, preferred_element_type=jnp.float32, **kw)


def frame_at(place, mine, frames):
    half = frames // 2
    return mine ^ (((place % half) << 1) | (place // half))


def place_of(frame, mine, frames):
    apart = mine ^ frame
    return (apart >> 1) + (apart & 1) * (frames // 2)


def query_frames(mine, frames):
    first = mine - (mine & 1)
    return (first, first + 1, jnp.minimum(first + 2, frames - 1), 0 * first)


def copies_of(pairs, sems, first):
    made = [pltpu.make_async_copy(src, dst, sems.at[first + i]) for i, (src, dst) in enumerate(pairs)]
    for copy in made:
        copy.start()
    return made


def span_of(j):
    return pl.ds(pl.multiple_of(j * CHUNK, CHUNK), CHUNK)


def spread_rows(made, count, channels, f):
    shift = made[count * channels + f : count * channels + f + 1, :]
    rest = (UROWS - channels, made.shape[1])
    first = lax.broadcasted_iota(jnp.int32, rest, 0) == 0
    return made[f * channels : (f + 1) * channels, :], jnp.where(first, jnp.broadcast_to(shift, rest), 0.0)


def packed_shifts(rows, feature):
    room = packed(len(rows)) - len(rows)
    if room:
        rows = rows + [jnp.zeros((room, feature), jnp.float32)]
    return jnp.concatenate(rows, axis=0).astype(jnp.bfloat16)


def packed(count):
    return -(-count // 16) * 16


def centred_patch(patch_ref):
    patch = patch_ref[...].astype(jnp.float32)
    return patch - jnp.mean(patch, axis=-1, keepdims=True)


def tables_kernel(frames, step_hbm, time_hbm, patch_hbm, qkv_hbm, q_gain_hbm, k_gain_hbm, out_hbm, head_hbm, tab_hbm, av_hbm, mix_hbm, sq_ref, step_ref, time_ref, patch_ref, head_ref, q_gain_ref, k_gain_ref, lhs, lhs_q, head_g, kv_ref, tab_ref, mix_ref, obuf, wbuf, sems):
    channels, feature = patch_ref.shape
    half = tab_ref.shape[2]
    count = half // CHUNK
    mine = lax.axis_index("queue")
    start = pl.multiple_of((mine & 1) * half, CHUNK)
    small = copies_of(
        (
            (step_hbm, step_ref),
            (patch_hbm, patch_ref),
            (time_hbm, time_ref),
            (head_hbm, head_ref),
            (q_gain_hbm.at[pl.ds(start, half)], q_gain_ref),
            (k_gain_hbm.at[pl.ds(start, half)], k_gain_ref),
        ),
        sems,
        0,
    )
    big = len(small)

    def fetch(n):
        base = jnp.where(n < count, feature, jnp.where(n < 2 * count, 2 * feature - half, -2 * half))
        at = pl.multiple_of(base + start + n * CHUNK, CHUNK)
        return pltpu.make_async_copy(
            qkv_hbm.at[:, pl.ds(at, CHUNK)], wbuf.at[:, span_of(n)], sems.at[big + n]
        )

    for n in range(2 * count):
        fetch(n).start()
    after = big + 3 * count
    out_copy = pltpu.make_async_copy(out_hbm.at[pl.ds(start, half), :], obuf, sems.at[after])
    for copy in small:
        copy.wait()
    centred = centred_patch(patch_ref)
    shifts = []
    for place in range(frames):
        level = step_ref[frame_at(place, mine, frames)]
        shifts.append(time_ref[0, pl.ds(level, 1), :])
        scale = time_ref[1, pl.ds(level, 1), :]
        lhs[place * channels : (place + 1) * channels, :] = (centred * (1.0 + scale)).astype(jnp.bfloat16)
    lhs[frames * channels :, :] = packed_shifts(shifts, feature)
    sq_ref[...] = jnp.zeros_like(sq_ref)
    high, low = split(centred)
    crossed = nt_dot(high, high) + nt_dot(high, low) + nt_dot(low, high)
    sq_ref[frames + GROUPS, :channels, :channels] = crossed / feature

    ratio = WIDE // CHUNK
    for n in range(ratio):
        fetch(n).wait()
    for n in range(2 * count, 3 * count):
        fetch(n).start()
    out_copy.start()

    def pair_step(j, carry):
        @pl.when(j > 0)
        def _():
            for n in range(ratio):
                fetch(j * ratio + n).wait()

        span = pl.ds(pl.multiple_of(j * WIDE, WIDE), WIDE)
        made = nn_dot(lhs[...], wbuf[:, span])
        for f in range(frames):
            top, tail = spread_rows(made, frames, channels, f)
            kv_ref[f, :channels, span] = top.astype(jnp.bfloat16)
            kv_ref[f, channels:, span] = tail.astype(jnp.bfloat16)
        return carry

    lax.fori_loop(0, 2 * half // WIDE, pair_step, 0)
    done = copies_of(
        ((kv_ref.at[:, :, :half], tab_hbm.at[:frames]), (kv_ref.at[:, :, half:], av_hbm)), sems, after + 1
    )
    for f in range(frames):
        block = kv_ref[f, :, :half]
        sq_ref[f] = nt_dot(block, block)
    which = query_frames(mine, frames)
    head = head_ref[...].astype(jnp.float32)
    for g, frame in enumerate(which):
        place = place_of(frame, mine, frames)
        at = pl.ds(pl.multiple_of(place * channels, 16), channels)
        lhs_q[g * channels : (g + 1) * channels, :] = lhs[at, :]
        gate = time_ref[2, pl.ds(step_ref[frame], 1), :]
        head_g[g * channels : (g + 1) * channels, :] = (head * gate).astype(jnp.bfloat16)
    shifts = [time_ref[0, pl.ds(step_ref[frame], 1), :] for frame in which]
    lhs_q[GROUPS * channels :, :] = packed_shifts(shifts, feature)
    sq_ref[frames + GROUPS + 1, :channels, :channels] = nt_dot(head_ref[...], patch_ref[...])


    for n in range(2 * count, 3 * count):
        fetch(n).wait()
    gain = (q_gain_ref[...] * k_gain_ref[...]).reshape(1, half)
    made = nn_dot(lhs_q[...], wbuf[:, 2 * half :])
    for g in range(GROUPS):
        both = jnp.concatenate(spread_rows(made, GROUPS, channels, g), axis=0)
        low = both.astype(jnp.bfloat16)
        sq_ref[frames + g] = nt_dot(low, low)
        tab_ref[g] = (both * gain).astype(jnp.bfloat16)
    done += copies_of(((tab_ref, tab_hbm.at[frames:]),), sems, after + 3)
    out_copy.wait()
    mixed = nt_dot(head_g[...], obuf[...]).astype(jnp.bfloat16)
    for g in range(GROUPS):
        mix_ref[g] = mixed[g * channels : (g + 1) * channels, :]
    done += copies_of(((mix_ref, mix_hbm),), sems, after + 4)
    for copy in done:
        copy.wait()


def split(x):
    high = x.astype(jnp.bfloat16)
    return high, (x - high.astype(jnp.float32)).astype(jnp.bfloat16)


def normed_rows(z, gram, square, feature):
    wide = z.astype(jnp.float32)
    gram_hi, gram_lo = split(gram)
    var = jnp.sum(wide * (nn_dot(gram_hi, z) + nn_dot(gram_lo, z)), axis=0, keepdims=True)
    scaled = wide * lax.rsqrt(jnp.maximum(var, 0.0) + EPS)
    tail = (UROWS - z.shape[0], z.shape[1])
    ones = (lax.broadcasted_iota(jnp.int32, tail, 0) == 0).astype(jnp.float32)
    rows = jnp.concatenate([scaled, ones], axis=0)
    rows_hi, rows_lo = split(rows)
    square_hi, square_lo = split(square)
    made = nn_dot(square_hi, rows_hi) + nn_dot(square_lo, rows_hi) + nn_dot(square_hi, rows_lo)
    mean_sq = jnp.sum(rows * made, axis=0, keepdims=True) / feature
    return rows, lax.rsqrt(jnp.maximum(mean_sq, 0.0) + EPS)


def latent_of(near_ref, far_ref, frame, frames):
    half = frames // 2
    place = place_of(frame, lax.axis_index("queue"), frames)
    inside = near_ref[jnp.minimum(place, half - 1)]
    outside = far_ref[jnp.maximum(place - half, 0)]
    return jnp.where(place < half, inside.astype(jnp.float32), outside.astype(jnp.float32))


def ask_kernel(frames, feature, near_ref, far_ref, tab_ref, sq_ref, sq_far, asked_ref, q_s):
    mine = lax.axis_index("queue")
    heads = q_s.shape[0]
    channels, tok = near_ref.shape[1:]
    gram = sq_ref[frames + GROUPS, :channels, :channels]
    scaling = HEAD_DIM ** (-0.5) * math.log2(math.e)
    for g, frame in enumerate(query_frames(mine, frames)):
        z = latent_of(near_ref, far_ref, frame, frames).astype(jnp.bfloat16)
        rows, factor = normed_rows(z, gram, sq_ref[frames + g] + sq_far[frames + g], feature)
        made = tn_dot(tab_ref[frames + g], (rows * (factor * scaling)).astype(jnp.bfloat16)).astype(jnp.bfloat16)
        for h in range(heads):
            q_s[h, :, g * tok : (g + 1) * tok] = made[h * HEAD_DIM : (h + 1) * HEAD_DIM, :]
    for h in range(heads):
        table = tab_ref[:frames, :, h * HEAD_DIM : (h + 1) * HEAD_DIM].reshape(frames * UROWS, HEAD_DIM)
        asked_ref[h] = nn_dot(table, q_s[h]).astype(jnp.bfloat16)


def each_portion(feature, z_s, asked_ref, squares, gram, emit, safe=False):
    heads = asked_ref.shape[0]
    groups, frames = z_s.shape[:2]
    ways = UNROLL if frames % UNROLL == 0 else 1
    for group in range(groups):

        def run(i, carry, group=group):
            items = []
            for way in range(ways):
                place = i * ways + way
                rows, factor = normed_rows(z_s[group, place], gram, squares(place), feature)
                key_rows = (rows * factor).T.astype(jnp.bfloat16)
                value_rows = rows.astype(jnp.bfloat16)
                items += [(h, place, key_rows, value_rows) for h in range(heads)]

            def scores_of(item):
                h, place, key_rows, _ = item
                return nn_dot(key_rows, asked_ref[h, rows_at(place), :])

            scores = scores_of(items[0])
            for n, (h, place, unused, value_rows) in enumerate(items):
                top = None
                if safe:
                    top = jnp.max(scores, axis=0, keepdims=True)
                    scores = scores - top
                weights = jnp.exp2(scores).astype(jnp.bfloat16)
                if n + 1 < len(items):
                    scores = scores_of(items[n + 1])
                emit(h, place, group, top, nn_dot(value_rows, weights))
            return carry

        lax.fori_loop(0, frames // ways, run, 0)


def squares_of(hk_ref, hk_far, frames):
    half = frames // 2
    return lambda place: hk_ref[place] + hk_far[lax.rem(place + half, frames)]


def rows_at(place):
    return pl.ds(pl.multiple_of(place * UROWS, 16), UROWS)


def attend_kernel(frames, levels, feature, step_ref, near_0, near_ref, far_0, far_ref, asked_ref, av_ref, mix_ref, sq_ref, sq_far, kept_ref, given_ref, z_s, m_s, o_s, part_s):
    mine = lax.axis_index("queue")
    core = mine & 1
    heads = asked_ref.shape[0]
    blocks, half, channels, tok = near_ref.shape
    gram = sq_ref[frames + GROUPS, :channels, :channels]
    squares = squares_of(sq_ref, sq_far, frames)
    step = z_s.shape[3] // tok
    for n in range(blocks + 1):
        at = slice((n % step) * tok, (n % step + 1) * tok)
        z_s[n // step, :half, :, at] = near_0[...] if n == 0 else near_ref[n - 1]
        z_s[n // step, half:, :, at] = far_0[...] if n == 0 else far_ref[n - 1]

    def emit(h, place, group, top, made):
        if group == 0:
            o_s[h, rows_at(place), :] = made
        else:
            o_s[h, rows_at(place), :] += made

    each_portion(feature, z_s, asked_ref, squares, gram, emit)

    def total_weight(h):
        total = o_s[h, channels : channels + 1, :]
        for i in range(1, frames):
            total = total + o_s[h, i * UROWS + channels : i * UROWS + channels + 1, :]
        return total

    flags = jnp.zeros((1, o_s.shape[2]), jnp.float32)
    for h in range(heads):
        total = total_weight(h)
        flags = jnp.maximum(flags, jnp.where((total > 2.0**-60) & (total < 2.0**100), 0.0, 1.0))

    @pl.when(jnp.max(flags) > 0.5)
    def _():
        m_s[...] = jnp.full_like(m_s, -1e30)
        o_s[...] = jnp.zeros_like(o_s)

        def shifted(h, place, group, top, made):
            row = pl.ds(place, 1)
            before = m_s[h, row, :]
            after = jnp.maximum(before, top)
            m_s[h, row, :] = after
            o_s[h, rows_at(place), :] = o_s[h, rows_at(place), :] * jnp.exp2(before - after) + made * jnp.exp2(
                top - after
            )

        each_portion(feature, z_s, asked_ref, squares, gram, shifted, safe=True)

        def rescale(i, carry):
            for h in range(heads):
                factor = jnp.exp2(m_s[h, pl.ds(i, 1), :] - jnp.max(m_s[h], axis=0, keepdims=True))
                o_s[h, rows_at(i), :] = o_s[h, rows_at(i), :] * factor
            return carry

        lax.fori_loop(0, frames, rescale, 0)

    lead = jnp.where(core == 0, 1.0, 0.0)
    totals = []
    skip_hi, skip_lo = split(sq_ref[frames + GROUPS + 1, :channels, :channels])
    for frame in query_frames(mine, frames):
        z = latent_of(near_0, far_0, frame, frames).astype(jnp.bfloat16)
        totals.append((nn_dot(skip_hi, z) + nn_dot(skip_lo, z)) * lead)
    for h in range(heads):
        span = slice(h * HEAD_DIM, (h + 1) * HEAD_DIM)
        mean_rows = (o_s[h] * (1.0 / total_weight(h))).astype(jnp.bfloat16)
        done = tn_dot(av_ref[:, :, span].reshape(frames * UROWS, HEAD_DIM), mean_rows).astype(jnp.bfloat16)
        for g in range(GROUPS):
            totals[g] = totals[g] + nn_dot(mix_ref[g, :, span], done[:, g * tok : (g + 1) * tok])
    for g in range(GROUPS):
        part_s[g] = totals[g]

    def drop(frame):
        before = jnp.where(frame > 0, step_ref[jnp.maximum(frame - 1, 0)], -1)
        return (before.astype(jnp.float32) - step_ref[frame].astype(jnp.float32)) / levels

    lat = channels // frames
    following = jnp.minimum(mine + 1, frames - 1)
    followed = jnp.minimum((mine ^ 1) + 1, frames - 1)
    kept_ref[:channels] = part_s[core]
    kept_ref[channels : 2 * channels] = (
        latent_of(near_0, far_0, following, frames) + drop(following) * part_s[core + 1]
    )
    given_ref[:channels] = part_s[1 - core]
    given_ref[channels : 2 * channels] = drop(followed) * part_s[2 - core]
    cleaned = drop(0 * mine) * part_s[GROUPS - 1]
    part_s[0] = cleaned + latent_of(near_0, far_0, 0 * mine, frames)
    part_s[1] = cleaned
    for i in range(lat):
        kept_ref[2 * channels + i : 2 * channels + i + 1, :] = part_s[0, pl.ds(mine * lat + i, 1), :]
        given_ref[2 * channels + i : 2 * channels + i + 1, :] = part_s[1, pl.ds((mine ^ 1) * lat + i, 1), :]


def finish_kernel(frames, kept_ref, got_ref, tail_ref, velocity_ref, next_ref, leaving_ref):
    channels = velocity_ref.shape[0]
    last = lax.axis_index("queue") == frames - 1
    velocity_ref[...] = kept_ref[:channels] + got_ref[:channels]
    arrived = kept_ref[channels : 2 * channels] + got_ref[channels : 2 * channels]
    next_ref[...] = jnp.where(last, tail_ref[...], arrived)
    leaving_ref[...] = kept_ref[2 * channels :] + got_ref[2 * channels :]


def swapped(value, axis, bit):
    peers = lax.axis_size(axis)
    return lax.ppermute(value, axis, [(i, i ^ bit) for i in range(peers)])


def per_device(
    latents,
    step_index,
    tail_noise,
    patch_weight,
    time_table,
    qkv_weight,
    q_gain,
    k_gain,
    out_weight,
    head_weight,
):
    return one_step(
        latents[0].T,
        step_index,
        tail_noise.T,
        patch_weight,
        time_table.transpose(1, 0, 2),
        qkv_weight,
        q_gain,
        k_gain,
        out_weight,
        head_weight.T,
    )


def shaped(*shapes):
    return [jax.ShapeDtypeStruct(shape, kind) for shape, kind in shapes]


def one_step(latent, step_index, tail, patch, times, qkv, q_gain, k_gain, out_w, head):
    channels, feature = patch.shape
    levels = times.shape[1]
    frames = lax.axis_size("queue")
    peers = lax.axis_size("tok")
    half = feature // 2
    heads = half // HEAD_DIM
    tok = latent.shape[1]
    count = half // CHUNK
    f32, bf16 = jnp.float32, jnp.bfloat16
    params = pltpu.CompilerParams(vmem_limit_bytes=(24 << 20) * max(1, frames // 8))

    made = (
        ((frames + GROUPS, UROWS, half), bf16),
        ((frames, UROWS, half), bf16),
        ((GROUPS, channels, half), bf16),
    )
    tab, av, mix, sq = pl.pallas_call(
        functools.partial(tables_kernel, frames),
        out_shape=shaped(*made, ((frames + GROUPS + 2, UROWS, UROWS), f32)),
        in_specs=[HBM] * 8,
        out_specs=[HBM] * 3 + [VMEM],
        scratch_shapes=[
            pltpu.SMEM((frames,), jnp.int32),
            pltpu.VMEM((3, levels, feature), f32),
            pltpu.VMEM((channels, feature), bf16),
            pltpu.VMEM((channels, feature), bf16),
            pltpu.VMEM((half,), f32),
            pltpu.VMEM((half,), f32),
            pltpu.VMEM((frames * channels + packed(frames), feature), bf16),
            pltpu.VMEM((GROUPS * channels + packed(GROUPS), feature), bf16),
            pltpu.VMEM((GROUPS * channels, feature), bf16),
        ]
        + [
            pltpu.VMEM((frames, UROWS, 2 * half), bf16),
            pltpu.VMEM((GROUPS, UROWS, half), bf16),
            pltpu.VMEM((GROUPS, channels, half), bf16),
            pltpu.VMEM((half, feature), bf16),
            pltpu.VMEM((feature, 3 * half), bf16),
            pltpu.SemaphoreType.DMA((3 * count + 11,)),
        ],
        compiler_params=pltpu.CompilerParams(vmem_limit_bytes=LIM_TAB),
        name="tables",
    )(step_index, times, patch, qkv, q_gain, k_gain, out_w, head)
    sq_far = swapped(sq, "queue", 1)

    own = latent.astype(bf16)[None]
    parts = [own]
    for apart in range(2, frames, 2):
        parts.append(swapped(own, "queue", apart))
    known = jnp.concatenate(parts, axis=0)
    own_far = swapped(known, "queue", 1)
    rows = GROUPS * tok
    (asked,) = pl.pallas_call(
        functools.partial(ask_kernel, frames, feature),
        out_shape=shaped(((heads, frames * UROWS, rows), bf16)),
        in_specs=[VMEM] * 5,
        out_specs=[VMEM],
        scratch_shapes=[pltpu.VMEM((heads, HEAD_DIM, rows), bf16)],
        compiler_params=params,
        cost_estimate=pl.CostEstimate(flops=10**9, bytes_accessed=4 * 10**6, transcendentals=0),
        name="ask",
    )(known, own_far, tab, sq, sq_far)

    parts = []
    for apart in range(1, peers):
        parts.append(swapped(known, "tok", apart)[None])
    near = jnp.concatenate(parts, axis=0)
    far = swapped(near, "queue", 1)

    held = min(peers, 4)
    share = channels // frames
    sent = (2 * channels + share, tok)
    kept, given = pl.pallas_call(
        functools.partial(attend_kernel, frames, levels, feature),
        out_shape=shaped((sent, f32), (sent, f32)),
        in_specs=[SMEM] + [VMEM] * 9,
        out_specs=[VMEM] * 2,
        scratch_shapes=[
            pltpu.VMEM((peers // held, frames, channels, held * tok), bf16),
            pltpu.VMEM((heads, frames, rows), f32),
            pltpu.VMEM((heads, frames * UROWS, rows), f32),
            pltpu.VMEM((GROUPS, channels, tok), f32),
        ],
        compiler_params=params,
        cost_estimate=pl.CostEstimate(flops=8 * 10**9, bytes_accessed=8 * 10**6, transcendentals=6 * 10**6),
        name="attend",
    )(step_index, known, near, own_far, far, asked, av, mix, sq, sq_far)
    got = swapped(given, "queue", 1)
    velocity, queue_next, leaving = pl.pallas_call(
        functools.partial(finish_kernel, frames),
        out_shape=shaped(((channels, tok), f32), ((channels, tok), f32), ((share, tok), f32)),
        in_specs=[VMEM] * 3,
        out_specs=[VMEM] * 3,
        compiler_params=pltpu.CompilerParams(vmem_limit_bytes=4 << 20),
        name="finish",
    )(kept, got, tail)
    return (velocity.T[None], queue_next.T[None], leaving)


def solution(mesh):
    placed = (P("queue", "tok", None), P(), P("tok", None), P(), P(), P(), P(), P(), P(), P())
    return jax.shard_map(
        per_device,
        mesh=mesh,
        in_specs=placed,
        out_specs=(P("queue", "tok", None), P("queue", "tok", None), P("queue", "tok")),
        check_vma=False,
    )
```
